32 devices in a mesh: row: 8 (over y, x, core), col: 4 (over z).
Axes of the slice: x: 2, y: 2, z: 4, core: 2. Of those that a mesh axis runs over, the one named last changes fastest.
Arguments:
- amplitudes: bfloat16 [256, 4096], P('row', 'col'), may hold values from -6 to 6
- integrals: bfloat16 [4096, 4096], P('col', 'row'), may hold values from -0.25 to 0.25
- occupied_irreps: int32 [256], replicated, may hold values from 0 to 7, as said below
- contracted_irreps: int32 [4096], P('col'), may hold values from 0 to 7
- output_irreps: int32 [4096], P('row'), may hold values from 0 to 7, as said below
Outputs:
- ladder: float32 [256, 4096], P('col', 'row')
The draws below stay inside these ranges and needn't reach their ends.
Inputs may be any that keep to these rules, and one draw needn't show every extreme that they name: `occupied_irreps`: in each aligned block of 64 occupied pairs, every irrep appears exactly 64 // 8 times. `output_irreps`: in each aligned block of 512 output pairs, every irrep appears exactly 512 // 8 times.
All inputs are finite; a program needn't handle non-finite values.
Results may differ from the reference program's by a relative error of at most 0.0003.
Values may be sent and summed in bfloat16 or wider, within the bound.
No kernel may reach another device: no remote copies, remote signals or barrier semaphores. Data moves between devices by JAX's collectives and lax.ppermute only.
A program may use at most 64 MiB of HBM per device.

```python
import jax
import jax.numpy as jnp

M_ROW = 512
IRREPS = 8
PAIRS = 256
PAIR_COL = 64
K = 4096
M = 4096


def balanced_labels(key, block, total):
    base = jnp.tile(jnp.arange(IRREPS, dtype=jnp.int32), block // IRREPS)
    keys = jax.random.split(key, total // block)
    shuffled = jax.vmap(lambda one_key: jax.random.permutation(one_key, base))(keys)
    return shuffled.reshape(total).astype(jnp.int32)


def draw_occupied_irreps(key, part):
    return balanced_labels(jax.random.fold_in(key, 11), PAIR_COL, PAIRS)


def draw_output_irreps(key, part):
    return balanced_labels(jax.random.fold_in(key, 23), M_ROW, M)


def set_ends(result, own_key, least, top_value):
    place = [jax.random.randint(jax.random.fold_in(own_key, axis), (), 0, length) for axis, length in enumerate(result.shape)]
    widest = result.shape.index(max(result.shape))
    beside = place[:widest] + [(place[widest] + 1) % result.shape[widest]] + place[widest + 1:]
    return result.at[tuple(place)].set(least).at[tuple(beside)].set(top_value)


def block_levels(stream_key, dims, cuts, least, top_value):
    level, own = 1.0, jax.random.fold_in(stream_key, 6)
    for position, shards_of in cuts:
        draws = jnp.exp(jax.random.uniform(jax.random.fold_in(own, position), (shards_of,), jnp.float32, least / len(cuts), top_value / len(cuts)))
        level = level * jnp.repeat(draws, dims[position] // shards_of).reshape([-1 if axis == position else 1 for axis in range(len(dims))])
    return level


def bell_draw(own_key, extent, width, reach, shards=(), kind=jnp.bfloat16):
    loudness = block_levels(own_key, extent, shards, -0.22, 0.18) if shards else 1.0
    array = jax.random.normal(own_key, extent, jnp.float32) * width * loudness
    return jnp.minimum(jnp.maximum(array, -reach), reach).astype(kind)


def setup_inputs(seed: int = 0) -> dict:
    splits = jax.random.split(jax.random.key(seed), 6)
    amplitudes = bell_draw(splits[0], (PAIRS, K), 1.0, 6.0, ((0, 8), (1, 4)))
    integrals = bell_draw(splits[1], (K, M), (K // IRREPS) ** -0.5, 0.25, ((0, 4), (1, 8)))
    occupied_irreps = draw_occupied_irreps(jax.random.fold_in(splits[5], 71), 0)
    contracted_irreps = set_ends(jax.random.randint(splits[3], (K,), 0, IRREPS), jax.random.fold_in(splits[3], 1), 0, IRREPS - 1).astype(jnp.int32)
    output_irreps = draw_output_irreps(jax.random.fold_in(splits[5], 71), 0)
    return {"amplitudes": amplitudes, "integrals": integrals, "occupied_irreps": occupied_irreps, "contracted_irreps": contracted_irreps, "output_irreps": output_irreps}


def reference(amplitudes, integrals, occupied_irreps, contracted_irreps, output_irreps):
    allowed = contracted_irreps[:, None] == output_irreps[None, :]
    masked = jnp.where(allowed, integrals, jnp.zeros_like(integrals))
    product = jnp.dot(amplitudes, masked, preferred_element_type=jnp.float32)
    matches = occupied_irreps[:, None] == output_irreps[None, :]
    return jnp.where(matches, product, jnp.zeros_like(product))
```

```python
import jax
import jax.numpy as jnp
from jax import lax
from jax.sharding import PartitionSpec as P

IRREPS = 8


def swap(x, axis, mask):
    count = lax.axis_size(axis)
    return lax.ppermute(x, axis, [(i, i ^ mask) for i in range(count)])


def ranks(labels, order):
    same = labels[:, None] == labels[None, :]
    before = order[None, :] < order[:, None]
    return jnp.sum((same & before).astype(jnp.int32), axis=1)


def body(amplitudes, integrals, occupied_irreps, contracted_irreps, output_irreps):
    rows, cols = lax.axis_size("row"), lax.axis_size("col")
    pairs = occupied_irreps.shape[0]
    own = amplitudes.shape[0]
    block = pairs // cols
    slots = block // IRREPS
    share = block // own
    row, col = lax.axis_index("row"), lax.axis_index("col")
    place, member = row // share, row % share

    raw, labels, order = [amplitudes], [], []
    step = 1
    while step < share:
        both = jnp.concatenate(raw, 0)
        raw.append(swap(both, "row", step))
        step *= 2
    raw = jnp.concatenate(raw, 0)
    for j in range(share):
        first = (member ^ j) * own
        labels.append(lax.dynamic_slice_in_dim(occupied_irreps, place * block + first, own, 0))
        order.append(first + jnp.arange(own, dtype=jnp.int32))
    labels, order = jnp.concatenate(labels), jnp.concatenate(order)
    rank = ranks(labels, order)
    pick = (rank[None, :] == jnp.arange(slots, dtype=jnp.int32)[:, None]).astype(jnp.bfloat16)
    kept = jnp.where(labels[:, None] == contracted_irreps[None, :], raw, jnp.zeros_like(raw))
    packed = jnp.dot(pick, kept, preferred_element_type=jnp.float32).astype(jnp.bfloat16)

    step = share
    while step < rows:
        packed = jnp.concatenate([packed, swap(packed, "row", step)], 0)
        step *= 2

    masked = jnp.where(contracted_irreps[:, None] == output_irreps[None, :], integrals, jnp.zeros_like(integrals))
    sums = jnp.dot(packed, masked, preferred_element_type=jnp.float32)
    turn = col ^ place
    parts = [lax.dynamic_slice_in_dim(sums, (turn ^ t) * slots, slots, 0) for t in range(cols)]
    step = cols // 2
    while step >= 1:
        got = swap(jnp.concatenate(parts[step:], 0), "col", step)
        parts = [parts[t] + got[t * slots : (t + 1) * slots] for t in range(step)]
        step //= 2
    total = parts[0]

    mine = lax.dynamic_slice_in_dim(occupied_irreps, col * block, block, 0)
    slot = ranks(mine, jnp.arange(block, dtype=jnp.int32))
    out = jnp.zeros((block, total.shape[1]), jnp.float32)
    match = mine[:, None] == output_irreps[None, :]
    for s in range(slots):
        out = jnp.where(match & (slot[:, None] == s), total[s][None, :], out)
    return out


def solution(mesh):
    return jax.shard_map(
        body,
        mesh=mesh,
        in_specs=(P("row", "col"), P("col", "row"), P(), P("col"), P("row")),
        out_specs=P("col", "row"),
        check_vma=False,
    )
```

```python
import jax
import jax.numpy as jnp
from jax import lax
from jax.sharding import PartitionSpec as P

IRREPS = 8


def swap(x, axis, mask):
    count = lax.axis_size(axis)
    return lax.ppermute(x, axis, [(i, i ^ mask) for i in range(count)])


def swap_both(x, flip, mask):
    rows, cols = lax.axis_size("row"), lax.axis_size("col")
    pairs = [(r * cols + c, (r ^ flip) * cols + (c ^ mask)) for r in range(rows) for c in range(cols)]
    return lax.ppermute(x, ("row", "col"), pairs)


def ranks(labels, order):
    same = labels[:, None] == labels[None, :]
    before = order[None, :] < order[:, None]
    return jnp.sum((same & before).astype(jnp.int32), axis=1)


def body(amplitudes, integrals, occupied_irreps, contracted_irreps, output_irreps):
    rows, cols = lax.axis_size("row"), lax.axis_size("col")
    pairs = occupied_irreps.shape[0]
    own = amplitudes.shape[0]
    block = pairs // cols
    slots = block // IRREPS
    share = block // own
    row, col = lax.axis_index("row"), lax.axis_index("col")
    place, member = row // share, row % share

    flip = 1 if share == 2 else 0

    raw, labels, order = [amplitudes], [], []
    step = 1
    while step < share:
        both = jnp.concatenate(raw, 0)
        raw.append(swap(both, "row", step))
        step *= 2
    raw = jnp.concatenate(raw, 0)
    for j in range(share):
        first = (member ^ j) * own
        labels.append(lax.dynamic_slice_in_dim(occupied_irreps, place * block + first, own, 0))
        order.append(first + jnp.arange(own, dtype=jnp.int32))
    labels, order = jnp.concatenate(labels), jnp.concatenate(order)
    rank = ranks(labels, order)
    pick = (rank[None, :] == jnp.arange(slots, dtype=jnp.int32)[:, None]).astype(jnp.bfloat16)
    kept = jnp.where(labels[:, None] == contracted_irreps[None, :], raw, jnp.zeros_like(raw))
    packed = jnp.dot(pick, kept, preferred_element_type=jnp.float32).astype(jnp.bfloat16)

    step = share
    while step < rows:
        packed = jnp.concatenate([packed, swap(packed, "row", step + flip)], 0)
        step *= 2

    masked = jnp.where(contracted_irreps[:, None] == output_irreps[None, :], integrals, jnp.zeros_like(integrals))
    masked = lax.optimization_barrier(masked)
    turn = col ^ place
    parts = []
    if flip:
        other = swap(masked, "row", 1)
    blocks = [lax.dynamic_slice_in_dim(packed, (turn ^ t) * slots, slots, 0) for t in range(cols)]
    odd = [bin(t).count("1") % 2 * flip for t in range(cols)]
    sums = [None] * cols
    for side in range(1 + flip):
        ours = [t for t in range(cols) if odd[t] == side]
        some = jnp.dot(jnp.concatenate([blocks[t] for t in ours], 0), other if side else masked, preferred_element_type=jnp.float32)
        for n, t in enumerate(ours):
            sums[t] = some[n * slots : (n + 1) * slots]
    step = 1
    while step < cols:
        got = swap_both(jnp.concatenate(sums[1::2], 0), flip, step)
        sums = [part + got[t * slots : (t + 1) * slots] for t, part in enumerate(sums[::2])]
        step *= 2
    total = sums[0]

    mine = lax.dynamic_slice_in_dim(occupied_irreps, col * block, block, 0)
    slot = ranks(mine, jnp.arange(block, dtype=jnp.int32))
    out = jnp.zeros((block, total.shape[1]), jnp.float32)
    match = mine[:, None] == output_irreps[None, :]
    for s in range(slots):
        out = jnp.where(match & (slot[:, None] == s), total[s][None, :], out)
    return out


def solution(mesh):
    return jax.shard_map(
        body,
        mesh=mesh,
        in_specs=(P("row", "col"), P("col", "row"), P(), P("col"), P("row")),
        out_specs=P("col", "row"),
        check_vma=False,
    )
```

```python
import functools

import jax
import jax.numpy as jnp
from jax import lax
from jax.experimental import pallas as pl
from jax.experimental.pallas import tpu as pltpu
from jax.sharding import PartitionSpec as P

IRREPS = 8
CORES, PLACES, COLS = 2, 4, 4


def in_hbm(x):
    return pltpu.with_memory_space_constraint(x, pltpu.HBM)


def in_vmem(x):
    return pltpu.with_memory_space_constraint(x, pltpu.VMEM)


def swap(x, axis, mask):
    count = lax.axis_size(axis)
    return lax.ppermute(x, axis, [(i, i ^ mask) for i in range(count)])


def ranks(labels, order):
    same = labels[:, None] == labels[None, :]
    before = order[None, :] < order[:, None]
    return jnp.sum((same & before).astype(jnp.int32), axis=1)


def general(amplitudes, integrals, occupied_irreps, contracted_irreps, output_irreps):
    rows, cols = lax.axis_size("row"), lax.axis_size("col")
    pairs = occupied_irreps.shape[0]
    own = amplitudes.shape[0]
    block = pairs // cols
    slots = block // IRREPS
    share = block // own
    row, col = lax.axis_index("row"), lax.axis_index("col")
    place, member = row // share, row % share

    raw, labels, order = [amplitudes], [], []
    step = 1
    while step < share:
        raw.append(swap(jnp.concatenate(raw, 0), "row", step))
        step *= 2
    raw = jnp.concatenate(raw, 0)
    for j in range(share):
        first = (member ^ j) * own
        labels.append(lax.dynamic_slice_in_dim(occupied_irreps, place * block + first, own, 0))
        order.append(first + jnp.arange(own, dtype=jnp.int32))
    labels, order = jnp.concatenate(labels), jnp.concatenate(order)
    rank = ranks(labels, order)
    pick = (rank[None, :] == jnp.arange(slots, dtype=jnp.int32)[:, None]).astype(jnp.bfloat16)
    kept = jnp.where(labels[:, None] == contracted_irreps[None, :], raw, jnp.zeros_like(raw))
    packed = jnp.dot(pick, kept, preferred_element_type=jnp.float32).astype(jnp.bfloat16)

    step = share
    while step < rows:
        packed = jnp.concatenate([packed, swap(packed, "row", step)], 0)
        step *= 2
    masked = jnp.where(contracted_irreps[:, None] == output_irreps[None, :], integrals, jnp.zeros_like(integrals))
    sums = jnp.dot(packed, masked, preferred_element_type=jnp.float32)
    turn = col ^ place
    parts = [lax.dynamic_slice_in_dim(sums, (turn ^ t) * slots, slots, 0) for t in range(cols)]
    step = 1
    while step < cols:
        got = swap(jnp.concatenate(parts[1::2], 0), "col", step)
        parts = [part + got[t * slots : (t + 1) * slots] for t, part in enumerate(parts[::2])]
        step *= 2
    total = parts[0]

    mine = lax.dynamic_slice_in_dim(occupied_irreps, col * block, block, 0)
    slot = ranks(mine, jnp.arange(block, dtype=jnp.int32))
    out = jnp.zeros((block, total.shape[1]), jnp.float32)
    match = mine[:, None] == output_irreps[None, :]
    for s in range(slots):
        out = jnp.where(match & (slot[:, None] == s), total[s][None, :], out)
    return out


def labels_and_ranks(occupied, place, block):
    labels = jnp.zeros((1, block), jnp.int32)
    for b in range(occupied.shape[1] // block):
        labels = jnp.where(place == b, occupied[:, b * block : (b + 1) * block], labels)
    lane = lax.broadcasted_iota(jnp.int32, (block, block), 1)
    sublane = lax.broadcasted_iota(jnp.int32, (block, block), 0)
    column = jnp.sum(jnp.where(lane == sublane, labels, 0), axis=1, keepdims=True)
    rank = jnp.sum(jnp.where((column == labels) & (sublane < lane), 1, 0), axis=0, keepdims=True)
    return column, rank


def pack_kernel(block, slots, occupied_ref, contracted_ref, amplitudes_ref, part_ref, gate_ref, pick_ref, occupied, contracted, own, sems):
    copies = [
        pltpu.make_async_copy(src, dst, sems.at[n])
        for n, (src, dst) in enumerate(((occupied_ref, occupied), (contracted_ref, contracted), (amplitudes_ref, own)))
    ]
    for copy in copies:
        copy.start()
    row = lax.axis_index("row")
    member = row % CORES
    rows = own.shape[0]
    copies[0].wait()
    column, rank = labels_and_ranks(occupied, row // CORES, block)
    slot = lax.broadcasted_iota(jnp.int32, (slots, rows), 0)
    ours = jnp.where(member == 0, rank[:, :rows], rank[:, rows:])
    theirs = jnp.where(member == 0, rank[:, rows:], rank[:, :rows])
    our_labels = jnp.where(member == 0, column[:rows], column[rows:])
    their_labels = jnp.where(member == 0, column[rows:], column[:rows])
    pick_ref[...] = jnp.where(slot == theirs, 1.0, 0.0).astype(jnp.bfloat16)
    copies[1].wait()
    gate_ref[...] = jnp.where(their_labels == contracted[...], 1.0, 0.0).astype(jnp.bfloat16)
    copies[2].wait()
    kept = jnp.where(our_labels == contracted[...], own[...].astype(jnp.float32), 0.0).astype(jnp.bfloat16)
    pick = jnp.where(slot == ours, 1.0, 0.0).astype(jnp.bfloat16)
    part_ref[...] = jnp.dot(pick, kept, preferred_element_type=jnp.float32)


def pack(occupied_irreps, contracted_irreps, amplitudes, block, slots):
    rows, depth = amplitudes.shape
    pairs = occupied_irreps.shape[0]
    return pl.pallas_call(
        functools.partial(pack_kernel, block, slots),
        out_shape=(
            pltpu.VMEM((slots, depth), jnp.float32),
            pltpu.VMEM((rows, depth), jnp.bfloat16),
            pltpu.VMEM((slots, rows), jnp.bfloat16),
        ),
        in_specs=[pl.BlockSpec(memory_space=pltpu.HBM)] * 3,
        out_specs=[pl.BlockSpec(memory_space=pltpu.VMEM)] * 3,
        scratch_shapes=[
            pltpu.VMEM((1, pairs), jnp.int32),
            pltpu.VMEM((1, depth), jnp.int32),
            pltpu.VMEM((rows, depth), jnp.bfloat16),
            pltpu.SemaphoreType.DMA((3,)),
        ],
        compiler_params=pltpu.CompilerParams(vmem_limit_bytes=8 << 20),
        cost_estimate=pl.CostEstimate(flops=1 << 20, bytes_accessed=1 << 18, transcendentals=0),
        name="pack",
    )(in_hbm(occupied_irreps.reshape(1, pairs)), in_hbm(contracted_irreps.reshape(1, depth)), in_hbm(amplitudes))


def stage_kernel(integrals_ref, occupied_ref, staged_ref, key_ref, occupied, sems):
    copies = [
        pltpu.make_async_copy(occupied_ref, occupied, sems.at[0]),
        pltpu.make_async_copy(integrals_ref, staged_ref, sems.at[1]),
    ]
    for copy in copies:
        copy.start()
    copies[0].wait()
    block = key_ref.shape[0]
    column, rank = labels_and_ranks(occupied[...], lax.axis_index("col"), block)
    lane = lax.broadcasted_iota(jnp.int32, (block, block), 1)
    sublane = lax.broadcasted_iota(jnp.int32, (block, block), 0)
    slot = jnp.sum(jnp.where(lane == sublane, rank, 0), axis=1, keepdims=True)
    key_ref[...] = jnp.broadcast_to(slot * IRREPS + column, key_ref.shape)
    copies[1].wait()


def stage(integrals, occupied_irreps, block):
    pairs = occupied_irreps.shape[0]
    return pl.pallas_call(
        stage_kernel,
        out_shape=(pltpu.VMEM(integrals.shape, integrals.dtype), pltpu.VMEM((block, 128), jnp.int32)),
        in_specs=[pl.BlockSpec(memory_space=pltpu.HBM)] * 2,
        out_specs=[pl.BlockSpec(memory_space=pltpu.VMEM)] * 2,
        scratch_shapes=[pltpu.VMEM((1, pairs), jnp.int32), pltpu.SemaphoreType.DMA((2,))],
        compiler_params=pltpu.CompilerParams(vmem_limit_bytes=8 << 20),
        cost_estimate=pl.CostEstimate(flops=0, bytes_accessed=4 * integrals.size, transcendentals=0),
        name="stage",
    )(in_hbm(integrals), in_hbm(occupied_irreps.reshape(1, pairs)))


def sums_kernel(slots, blocks_refs, contracted_ref, outputs_ref, other_outputs_ref, integrals_ref, other_ref, send_ref, far_ref, keep_ref):
    row, col = lax.axis_index("row"), lax.axis_index("col")
    place, member = row // CORES, row % CORES
    contracted = contracted_ref[...]
    blocks = [ref[...].astype(jnp.float32) for ref in blocks_refs]

    def block(t):
        offset = col ^ place ^ t
        turned = jnp.where((offset == 1) | (offset == 2), offset ^ ((1 - member) * 3), offset)
        chosen = blocks[0]
        for n in range(1, PLACES):
            chosen = jnp.where(turned == n, blocks[n], chosen)
        return chosen

    def product(rows, weights, outputs):
        spread = jnp.concatenate([jnp.where(contracted == g, rows, 0.0) for g in range(IRREPS)], axis=0)
        each = jnp.dot(spread.astype(jnp.bfloat16), weights, preferred_element_type=jnp.float32)
        total = jnp.zeros((2 * slots, each.shape[1]), jnp.float32)
        for g in range(IRREPS):
            total = jnp.where(outputs == g, each[g * 2 * slots : (g + 1) * 2 * slots], total)
        return total

    sent = block(1 + member)
    theirs = product(jnp.concatenate([sent, block(3)], 0), other_ref[...], other_outputs_ref[...])
    send_ref[:slots] = theirs[:slots]
    far_ref[...] = theirs[slots:]
    ours = product(jnp.concatenate([sent, block(0)], 0), integrals_ref[...], outputs_ref[...])
    send_ref[slots:] = ours[:slots]
    keep_ref[...] = ours[slots:]


def sums(blocks, contracted, outputs, other_outputs, integrals, other, slots):
    depth, width = integrals.shape

    def kernel(b0, b1, b2, b3, *refs):
        sums_kernel(slots, (b0, b1, b2, b3), *refs)

    args = [*blocks, contracted.reshape(1, depth), outputs.reshape(1, width), other_outputs.reshape(1, width), integrals, other]
    return pl.pallas_call(
        kernel,
        out_shape=(
            pltpu.VMEM((2 * slots, width), jnp.float32),
            pltpu.VMEM((slots, width), jnp.float32),
            pltpu.VMEM((slots, width), jnp.float32),
        ),
        in_specs=[pl.BlockSpec(memory_space=pltpu.VMEM)] * len(args),
        out_specs=[pl.BlockSpec(memory_space=pltpu.VMEM)] * 3,
        compiler_params=pltpu.CompilerParams(vmem_limit_bytes=16 << 20),
        cost_estimate=pl.CostEstimate(flops=1 << 28, bytes_accessed=1 << 21, transcendentals=0),
        name="sums",
    )(*[in_vmem(x) for x in args])


def expand_kernel(keep_ref, got_ref, far_ref, too_ref, key_ref, outputs_ref, out_ref, staged, sems):
    slots, width = keep_ref.shape
    block = key_ref.shape[0]
    outputs = outputs_ref[...]
    total = (keep_ref[...] + got_ref[:slots]) + (far_ref[...] + too_ref[...])
    pieces = sems.shape[0]
    size = block // pieces
    copies = []
    for n in range(pieces):
        rows = slice(n * size, (n + 1) * size)
        key = key_ref[rows, :1]
        out = jnp.zeros((size, width), jnp.float32)
        for s in range(slots):
            out = jnp.where(key == outputs + s * IRREPS, total[s : s + 1], out)
        staged[rows] = out
        copy = pltpu.make_async_copy(staged.at[rows], out_ref.at[rows], sems.at[n])
        copy.start()
        copies.append(copy)
    for copy in copies:
        copy.wait()


def expand(keep, got, far, too, key, outputs, pieces=2):
    slots, width = keep.shape
    block = key.shape[0]
    args = [keep, got, far, too, key, outputs.reshape(1, width)]
    return pl.pallas_call(
        expand_kernel,
        out_shape=pltpu.HBM((block, width), jnp.float32),
        in_specs=[pl.BlockSpec(memory_space=pltpu.VMEM)] * len(args),
        out_specs=pl.BlockSpec(memory_space=pltpu.HBM),
        scratch_shapes=[pltpu.VMEM((block, width), jnp.float32), pltpu.SemaphoreType.DMA((pieces,))],
        compiler_params=pltpu.CompilerParams(vmem_limit_bytes=8 << 20),
        cost_estimate=pl.CostEstimate(flops=1 << 20, bytes_accessed=1 << 18, transcendentals=0),
        name="expand",
    )(*[in_vmem(x) for x in args])


def move(x, target):
    pairs = []
    for r in range(PLACES * CORES):
        for c in range(COLS):
            place, member, col = target(r // CORES, r % CORES, c)
            pairs.append((r * COLS + c, (place * CORES + member) * COLS + col))
    return lax.ppermute(x, ("row", "col"), pairs)


def quad(amplitudes, integrals, occupied_irreps, contracted_irreps, output_irreps):
    own = amplitudes.shape[0]
    block = own * CORES
    slots = block // IRREPS
    sibling = lambda p, m, c: (p, 1 - m, c)

    raw = move(amplitudes, sibling)
    part, gate, pick = pack(occupied_irreps, contracted_irreps, amplitudes, block, slots)
    raw, part, late_integrals, late_outputs = lax.optimization_barrier((raw, part, integrals, output_irreps))
    other = move(late_integrals, sibling)
    other_outputs = move(late_outputs, sibling)
    packed = (part + jnp.dot(pick, raw * gate, preferred_element_type=jnp.float32)).astype(jnp.bfloat16)

    packed, late_integrals = lax.optimization_barrier((packed, integrals))
    side = move(packed, lambda p, m, c: (p ^ (1 + m), 1 - m, c))
    far = move(packed, lambda p, m, c: (p ^ 3, 1 - m, c))
    staged, key = stage(late_integrals, occupied_irreps, block)
    side, staged = lax.optimization_barrier((side, staged))
    side_too = move(side, sibling)
    send, send_far, keep = sums(
        (packed, side, side_too, far), contracted_irreps, output_irreps, other_outputs, staged, other, slots
    )
    got = move(send, lambda p, m, c: (p, 1 - m, c ^ (1 + m)))
    got_far = move(send_far, lambda p, m, c: (p, 1 - m, c ^ 3))
    got_too = move(got[slots:], sibling)
    return expand(keep, got, got_far, got_too, key, output_irreps)


def solution(mesh):
    small = mesh.shape["row"] == PLACES * CORES and mesh.shape["col"] == COLS
    return jax.shard_map(
        quad if small else general,
        mesh=mesh,
        in_specs=(P("row", "col"), P("col", "row"), P(), P("col"), P("row")),
        out_specs=P("col", "row"),
        check_vma=False,
    )
```

```python
import functools

import jax
import jax.numpy as jnp
from jax import lax
from jax.experimental import pallas as pl
from jax.experimental.pallas import tpu as pltpu
from jax.sharding import PartitionSpec as P

IRREPS = 8
CORES, PLACES, COLS = 2, 4, 4


def in_hbm(x):
    return pltpu.with_memory_space_constraint(x, pltpu.HBM)


def in_vmem(x):
    return pltpu.with_memory_space_constraint(x, pltpu.VMEM)


def swap(x, axis, mask):
    count = lax.axis_size(axis)
    return lax.ppermute(x, axis, [(i, i ^ mask) for i in range(count)])


def ranks(labels, order):
    same = labels[:, None] == labels[None, :]
    before = order[None, :] < order[:, None]
    return jnp.sum((same & before).astype(jnp.int32), axis=1)


def general(amplitudes, integrals, occupied_irreps, contracted_irreps, output_irreps):
    rows, cols = lax.axis_size("row"), lax.axis_size("col")
    pairs = occupied_irreps.shape[0]
    own = amplitudes.shape[0]
    block = pairs // cols
    slots = block // IRREPS
    share = block // own
    row, col = lax.axis_index("row"), lax.axis_index("col")
    place, member = row // share, row % share

    raw, labels, order = [amplitudes], [], []
    step = 1
    while step < share:
        raw.append(swap(jnp.concatenate(raw, 0), "row", step))
        step *= 2
    raw = jnp.concatenate(raw, 0)
    for j in range(share):
        first = (member ^ j) * own
        labels.append(lax.dynamic_slice_in_dim(occupied_irreps, place * block + first, own, 0))
        order.append(first + jnp.arange(own, dtype=jnp.int32))
    labels, order = jnp.concatenate(labels), jnp.concatenate(order)
    rank = ranks(labels, order)
    pick = (rank[None, :] == jnp.arange(slots, dtype=jnp.int32)[:, None]).astype(jnp.bfloat16)
    kept = jnp.where(labels[:, None] == contracted_irreps[None, :], raw, jnp.zeros_like(raw))
    packed = jnp.dot(pick, kept, preferred_element_type=jnp.float32).astype(jnp.bfloat16)

    step = share
    while step < rows:
        packed = jnp.concatenate([packed, swap(packed, "row", step)], 0)
        step *= 2
    masked = jnp.where(contracted_irreps[:, None] == output_irreps[None, :], integrals, jnp.zeros_like(integrals))
    sums = jnp.dot(packed, masked, preferred_element_type=jnp.float32)
    turn = col ^ place
    parts = [lax.dynamic_slice_in_dim(sums, (turn ^ t) * slots, slots, 0) for t in range(cols)]
    step = 1
    while step < cols:
        got = swap(jnp.concatenate(parts[1::2], 0), "col", step)
        parts = [part + got[t * slots : (t + 1) * slots] for t, part in enumerate(parts[::2])]
        step *= 2
    total = parts[0]

    mine = lax.dynamic_slice_in_dim(occupied_irreps, col * block, block, 0)
    slot = ranks(mine, jnp.arange(block, dtype=jnp.int32))
    out = jnp.zeros((block, total.shape[1]), jnp.float32)
    match = mine[:, None] == output_irreps[None, :]
    for s in range(slots):
        out = jnp.where(match & (slot[:, None] == s), total[s][None, :], out)
    return out


def labels_and_ranks(occupied, place, block):
    labels = jnp.zeros((1, block), jnp.int32)
    for b in range(occupied.shape[1] // block):
        labels = jnp.where(place == b, occupied[:, b * block : (b + 1) * block], labels)
    lane = lax.broadcasted_iota(jnp.int32, (block, block), 1)
    sublane = lax.broadcasted_iota(jnp.int32, (block, block), 0)
    column = jnp.sum(jnp.where(lane == sublane, labels, 0), axis=1, keepdims=True)
    rank = jnp.sum(jnp.where((column == labels) & (sublane < lane), 1, 0), axis=0, keepdims=True)
    return column, rank


def pack_kernel(block, slots, occupied_ref, contracted_ref, amplitudes_ref, part_ref, gate_ref, pick_ref, occupied, contracted, own, sems):
    copies = [
        pltpu.make_async_copy(src, dst, sems.at[n])
        for n, (src, dst) in enumerate(((occupied_ref, occupied), (contracted_ref, contracted), (amplitudes_ref, own)))
    ]
    for copy in copies:
        copy.start()
    row = lax.axis_index("row")
    member = row % CORES
    rows = own.shape[0]
    copies[0].wait()
    column, rank = labels_and_ranks(occupied, row // CORES, block)
    slot = lax.broadcasted_iota(jnp.int32, (slots, rows), 0)
    ours = jnp.where(member == 0, rank[:, :rows], rank[:, rows:])
    theirs = jnp.where(member == 0, rank[:, rows:], rank[:, :rows])
    our_labels = jnp.where(member == 0, column[:rows], column[rows:])
    their_labels = jnp.where(member == 0, column[rows:], column[:rows])
    pick_ref[...] = jnp.where(slot == theirs, 1.0, 0.0).astype(jnp.bfloat16)
    copies[1].wait()
    gate_ref[...] = jnp.where(their_labels == contracted[...], 1.0, 0.0).astype(jnp.bfloat16)
    copies[2].wait()
    kept = jnp.where(our_labels == contracted[...], own[...].astype(jnp.float32), 0.0).astype(jnp.bfloat16)
    pick = jnp.where(slot == ours, 1.0, 0.0).astype(jnp.bfloat16)
    part_ref[...] = jnp.dot(pick, kept, preferred_element_type=jnp.float32)


def pack(occupied_irreps, contracted_irreps, amplitudes, block, slots):
    rows, depth = amplitudes.shape
    pairs = occupied_irreps.shape[0]
    return pl.pallas_call(
        functools.partial(pack_kernel, block, slots),
        out_shape=(
            pltpu.VMEM((slots, depth), jnp.float32),
            pltpu.VMEM((rows, depth), jnp.bfloat16),
            pltpu.VMEM((slots, rows), jnp.bfloat16),
        ),
        in_specs=[pl.BlockSpec(memory_space=pltpu.HBM)] * 3,
        out_specs=[pl.BlockSpec(memory_space=pltpu.VMEM)] * 3,
        scratch_shapes=[
            pltpu.VMEM((1, pairs), jnp.int32),
            pltpu.VMEM((1, depth), jnp.int32),
            pltpu.VMEM((rows, depth), jnp.bfloat16),
            pltpu.SemaphoreType.DMA((3,)),
        ],
        compiler_params=pltpu.CompilerParams(vmem_limit_bytes=8 << 20),
        cost_estimate=pl.CostEstimate(flops=1 << 20, bytes_accessed=1 << 18, transcendentals=0),
        name="pack",
    )(in_hbm(occupied_irreps.reshape(1, pairs)), in_hbm(contracted_irreps.reshape(1, depth)), in_hbm(amplitudes))


def stage_kernel(integrals_ref, occupied_ref, staged_ref, key_ref, occupied, sems):
    copies = [
        pltpu.make_async_copy(occupied_ref, occupied, sems.at[0]),
        pltpu.make_async_copy(integrals_ref, staged_ref, sems.at[1]),
    ]
    for copy in copies:
        copy.start()
    copies[0].wait()
    block = key_ref.shape[0]
    column, rank = labels_and_ranks(occupied[...], lax.axis_index("col"), block)
    lane = lax.broadcasted_iota(jnp.int32, (block, block), 1)
    sublane = lax.broadcasted_iota(jnp.int32, (block, block), 0)
    slot = jnp.sum(jnp.where(lane == sublane, rank, 0), axis=1, keepdims=True)
    key_ref[...] = jnp.broadcast_to(slot * IRREPS + column, key_ref.shape)
    copies[1].wait()


def stage(integrals, occupied_irreps, block):
    pairs = occupied_irreps.shape[0]
    return pl.pallas_call(
        stage_kernel,
        out_shape=(pltpu.VMEM(integrals.shape, integrals.dtype), pltpu.VMEM((block, 128), jnp.int32)),
        in_specs=[pl.BlockSpec(memory_space=pltpu.HBM)] * 2,
        out_specs=[pl.BlockSpec(memory_space=pltpu.VMEM)] * 2,
        scratch_shapes=[pltpu.VMEM((1, pairs), jnp.int32), pltpu.SemaphoreType.DMA((2,))],
        compiler_params=pltpu.CompilerParams(vmem_limit_bytes=8 << 20),
        cost_estimate=pl.CostEstimate(flops=0, bytes_accessed=4 * integrals.size, transcendentals=0),
        name="stage",
    )(in_hbm(integrals), in_hbm(occupied_irreps.reshape(1, pairs)))


def sums_kernel(slots, blocks_refs, contracted_ref, outputs_ref, other_outputs_ref, integrals_ref, other_ref, send_ref, far_ref, keep_ref):
    row, col = lax.axis_index("row"), lax.axis_index("col")
    place, member = row // CORES, row % CORES
    contracted = contracted_ref[...]
    blocks = [ref[...].astype(jnp.float32) for ref in blocks_refs]

    def block(t):
        offset = ((col + t) % COLS) ^ place
        turned = jnp.where((offset == 1) | (offset == 2), offset ^ ((1 - member) * 3), offset)
        chosen = blocks[0]
        for n in range(1, PLACES):
            chosen = jnp.where(turned == n, blocks[n], chosen)
        return chosen

    def product(rows, weights, outputs):
        spread = jnp.concatenate([jnp.where(contracted == g, rows, 0.0) for g in range(IRREPS)], axis=0)
        each = jnp.dot(spread.astype(jnp.bfloat16), weights, preferred_element_type=jnp.float32)
        total = jnp.zeros((2 * slots, each.shape[1]), jnp.float32)
        for g in range(IRREPS):
            total = jnp.where(outputs == g, each[g * 2 * slots : (g + 1) * 2 * slots], total)
        return total

    sent = block(1 + member)
    theirs = product(jnp.concatenate([sent, block(3)], 0), other_ref[...], other_outputs_ref[...])
    send_ref[:slots] = theirs[:slots]
    far_ref[...] = theirs[slots:]
    ours = product(jnp.concatenate([sent, block(0)], 0), integrals_ref[...], outputs_ref[...])
    send_ref[slots:] = ours[:slots]
    keep_ref[...] = ours[slots:]


def sums(blocks, contracted, outputs, other_outputs, integrals, other, slots):
    depth, width = integrals.shape

    def kernel(b0, b1, b2, b3, *refs):
        sums_kernel(slots, (b0, b1, b2, b3), *refs)

    args = [*blocks, contracted.reshape(1, depth), outputs.reshape(1, width), other_outputs.reshape(1, width), integrals, other]
    return pl.pallas_call(
        kernel,
        out_shape=(
            pltpu.VMEM((2 * slots, width), jnp.float32),
            pltpu.VMEM((slots, width), jnp.float32),
            pltpu.VMEM((slots, width), jnp.float32),
        ),
        in_specs=[pl.BlockSpec(memory_space=pltpu.VMEM)] * len(args),
        out_specs=[pl.BlockSpec(memory_space=pltpu.VMEM)] * 3,
        compiler_params=pltpu.CompilerParams(vmem_limit_bytes=16 << 20),
        cost_estimate=pl.CostEstimate(flops=1 << 28, bytes_accessed=1 << 21, transcendentals=0),
        name="sums",
    )(*[in_vmem(x) for x in args])


def expand_kernel(keep_ref, got_ref, far_ref, too_ref, key_ref, outputs_ref, out_ref, staged, sems):
    slots, width = keep_ref.shape
    block = key_ref.shape[0]
    outputs = outputs_ref[...]
    total = (keep_ref[...] + got_ref[:slots]) + (far_ref[...] + too_ref[...])
    pieces = sems.shape[0]
    size = block // pieces
    copies = []
    for n in range(pieces):
        rows = slice(n * size, (n + 1) * size)
        key = key_ref[rows, :1]
        out = jnp.zeros((size, width), jnp.float32)
        for s in range(slots):
            out = jnp.where(key == outputs + s * IRREPS, total[s : s + 1], out)
        staged[rows] = out
        copy = pltpu.make_async_copy(staged.at[rows], out_ref.at[rows], sems.at[n])
        copy.start()
        copies.append(copy)
    for copy in copies:
        copy.wait()


def expand(keep, got, far, too, key, outputs, pieces=2):
    slots, width = keep.shape
    block = key.shape[0]
    args = [keep, got, far, too, key, outputs.reshape(1, width)]
    return pl.pallas_call(
        expand_kernel,
        out_shape=pltpu.HBM((block, width), jnp.float32),
        in_specs=[pl.BlockSpec(memory_space=pltpu.VMEM)] * len(args),
        out_specs=pl.BlockSpec(memory_space=pltpu.HBM),
        scratch_shapes=[pltpu.VMEM((block, width), jnp.float32), pltpu.SemaphoreType.DMA((pieces,))],
        compiler_params=pltpu.CompilerParams(vmem_limit_bytes=8 << 20),
        cost_estimate=pl.CostEstimate(flops=1 << 20, bytes_accessed=1 << 18, transcendentals=0),
        name="expand",
    )(*[in_vmem(x) for x in args])


def move(x, target):
    pairs = []
    for r in range(PLACES * CORES):
        for c in range(COLS):
            place, member, col = target(r // CORES, r % CORES, c)
            pairs.append((r * COLS + c, (place * CORES + member) * COLS + col))
    return lax.ppermute(x, ("row", "col"), pairs)


def quad(amplitudes, integrals, occupied_irreps, contracted_irreps, output_irreps):
    own = amplitudes.shape[0]
    block = own * CORES
    slots = block // IRREPS
    sibling = lambda p, m, c: (p, 1 - m, c)

    raw = move(amplitudes, sibling)
    part, gate, pick = pack(occupied_irreps, contracted_irreps, amplitudes, block, slots)
    raw, part, late_integrals, late_outputs = lax.optimization_barrier((raw, part, integrals, output_irreps))
    other = move(late_integrals, sibling)
    other_outputs = move(late_outputs, sibling)
    packed = (part + jnp.dot(pick, raw * gate, preferred_element_type=jnp.float32)).astype(jnp.bfloat16)

    packed, late_integrals = lax.optimization_barrier((packed, integrals))
    side = move(packed, lambda p, m, c: (p ^ (1 + m), 1 - m, c))
    far = move(packed, lambda p, m, c: (p ^ 3, 1 - m, c))
    staged, key = stage(late_integrals, occupied_irreps, block)
    side, staged = lax.optimization_barrier((side, staged))
    side_too = move(side, sibling)
    send, send_far, keep = sums(
        (packed, side, side_too, far), contracted_irreps, output_irreps, other_outputs, staged, other, slots
    )
    got = move(send, lambda p, m, c: (p, 1 - m, (c + 1 + m) % COLS))
    got_far = move(send_far, lambda p, m, c: (p, 1 - m, (c + 3) % COLS))
    got_too = move(got[slots:], sibling)
    return expand(keep, got, got_far, got_too, key, output_irreps)


def solution(mesh):
    small = mesh.shape["row"] == PLACES * CORES and mesh.shape["col"] == COLS
    return jax.shard_map(
        quad if small else general,
        mesh=mesh,
        in_specs=(P("row", "col"), P("col", "row"), P(), P("col"), P("row")),
        out_specs=P("col", "row"),
        check_vma=False,
    )
```

```python
import functools

import jax
import jax.numpy as jnp
from jax import lax
from jax.experimental import pallas as pl
from jax.experimental.pallas import tpu as pltpu
from jax.sharding import PartitionSpec as P

IRREPS = 8
CORES, PLACES, COLS = 2, 4, 4


def in_hbm(x):
    return pltpu.with_memory_space_constraint(x, pltpu.HBM)


def in_vmem(x):
    return pltpu.with_memory_space_constraint(x, pltpu.VMEM)


def swap(x, axis, mask):
    count = lax.axis_size(axis)
    return lax.ppermute(x, axis, [(i, i ^ mask) for i in range(count)])


def ranks(labels, order):
    same = labels[:, None] == labels[None, :]
    before = order[None, :] < order[:, None]
    return jnp.sum((same & before).astype(jnp.int32), axis=1)


def general(amplitudes, integrals, occupied_irreps, contracted_irreps, output_irreps):
    rows, cols = lax.axis_size("row"), lax.axis_size("col")
    pairs = occupied_irreps.shape[0]
    own = amplitudes.shape[0]
    block = pairs // cols
    slots = block // IRREPS
    share = block // own
    row, col = lax.axis_index("row"), lax.axis_index("col")
    place, member = row // share, row % share

    raw, labels, order = [amplitudes], [], []
    step = 1
    while step < share:
        raw.append(swap(jnp.concatenate(raw, 0), "row", step))
        step *= 2
    raw = jnp.concatenate(raw, 0)
    for j in range(share):
        first = (member ^ j) * own
        labels.append(lax.dynamic_slice_in_dim(occupied_irreps, place * block + first, own, 0))
        order.append(first + jnp.arange(own, dtype=jnp.int32))
    labels, order = jnp.concatenate(labels), jnp.concatenate(order)
    rank = ranks(labels, order)
    pick = (rank[None, :] == jnp.arange(slots, dtype=jnp.int32)[:, None]).astype(jnp.bfloat16)
    kept = jnp.where(labels[:, None] == contracted_irreps[None, :], raw, jnp.zeros_like(raw))
    packed = jnp.dot(pick, kept, preferred_element_type=jnp.float32).astype(jnp.bfloat16)

    step = share
    while step < rows:
        packed = jnp.concatenate([packed, swap(packed, "row", step)], 0)
        step *= 2
    masked = jnp.where(contracted_irreps[:, None] == output_irreps[None, :], integrals, jnp.zeros_like(integrals))
    sums = jnp.dot(packed, masked, preferred_element_type=jnp.float32)
    turn = col ^ place
    parts = [lax.dynamic_slice_in_dim(sums, (turn ^ t) * slots, slots, 0) for t in range(cols)]
    step = 1
    while step < cols:
        got = swap(jnp.concatenate(parts[1::2], 0), "col", step)
        parts = [part + got[t * slots : (t + 1) * slots] for t, part in enumerate(parts[::2])]
        step *= 2
    total = parts[0]

    mine = lax.dynamic_slice_in_dim(occupied_irreps, col * block, block, 0)
    slot = ranks(mine, jnp.arange(block, dtype=jnp.int32))
    out = jnp.zeros((block, total.shape[1]), jnp.float32)
    match = mine[:, None] == output_irreps[None, :]
    for s in range(slots):
        out = jnp.where(match & (slot[:, None] == s), total[s][None, :], out)
    return out


def keys(occupied, place, block):
    slots = block // IRREPS
    labels = jnp.zeros((1, block), jnp.int32)
    for b in range(occupied.shape[1] // block):
        labels = jnp.where(place == b, occupied[:, b * block : (b + 1) * block], labels)
    irrep = lax.broadcasted_iota(jnp.int32, (IRREPS, block), 0)
    same = jnp.where(labels == irrep, 1.0, 0.0)
    lane = lax.broadcasted_iota(jnp.int32, (block, block), 1)
    sublane = lax.broadcasted_iota(jnp.int32, (block, block), 0)
    before = jnp.where(sublane < lane, 1.0, 0.0).astype(jnp.bfloat16)
    counts = jnp.dot(same.astype(jnp.bfloat16), before, preferred_element_type=jnp.float32)
    rank = jnp.sum(same * counts, axis=0, keepdims=True)
    return labels * slots + rank.astype(jnp.int32)


def pack_kernel(block, occupied_ref, contracted_ref, amplitudes_ref, order_ref, contracted_out, own_out, occupied, sems):
    copies = [
        pltpu.make_async_copy(src, dst, sems.at[n])
        for n, (src, dst) in enumerate(
            ((occupied_ref, occupied), (contracted_ref, contracted_out), (amplitudes_ref, own_out))
        )
    ]
    for copy in copies:
        copy.start()
    copies[0].wait()
    key = keys(occupied[...], lax.axis_index("row") // CORES, block)
    sublane = lax.broadcasted_iota(jnp.int32, (block, block), 0)
    order_ref[...] = jnp.where(key == sublane, 1.0, 0.0).astype(jnp.bfloat16)
    for copy in copies[1:]:
        copy.wait()


def pack(occupied_irreps, contracted_irreps, amplitudes, block):
    rows, depth = amplitudes.shape
    pairs = occupied_irreps.shape[0]
    return pl.pallas_call(
        functools.partial(pack_kernel, block),
        out_shape=(
            pltpu.VMEM((block, block), jnp.bfloat16),
            pltpu.VMEM((1, depth), jnp.int32),
            pltpu.VMEM((rows, depth), jnp.bfloat16),
        ),
        in_specs=[pl.BlockSpec(memory_space=pltpu.HBM)] * 3,
        out_specs=[pl.BlockSpec(memory_space=pltpu.VMEM)] * 3,
        scratch_shapes=[pltpu.VMEM((1, pairs), jnp.int32), pltpu.SemaphoreType.DMA((3,))],
        compiler_params=pltpu.CompilerParams(vmem_limit_bytes=8 << 20),
        cost_estimate=pl.CostEstimate(flops=1 << 20, bytes_accessed=1 << 18, transcendentals=0),
        name="pack",
    )(in_hbm(occupied_irreps.reshape(1, pairs)), in_hbm(contracted_irreps.reshape(1, depth)), in_hbm(amplitudes))


def fold_kernel(slots, order_ref, contracted_ref, own_ref, raw_ref, packed_ref):
    first = lax.axis_index("row") % CORES == 0
    own, raw = own_ref[...], raw_ref[...]
    rows = jnp.concatenate([jnp.where(first, own, raw), jnp.where(first, raw, own)], axis=0)
    ordered = jnp.dot(order_ref[...], rows, preferred_element_type=jnp.float32)
    contracted = contracted_ref[...]
    packed = jnp.zeros((slots, contracted.shape[1]), jnp.float32)
    for g in range(IRREPS):
        packed = jnp.where(contracted == g, ordered[g * slots : (g + 1) * slots], packed)
    packed_ref[...] = packed.astype(jnp.bfloat16)


def fold(order, contracted, own, raw, slots):
    args = [order, contracted, own, raw]
    return pl.pallas_call(
        functools.partial(fold_kernel, slots),
        out_shape=pltpu.VMEM((slots, own.shape[1]), jnp.bfloat16),
        in_specs=[pl.BlockSpec(memory_space=pltpu.VMEM)] * len(args),
        out_specs=pl.BlockSpec(memory_space=pltpu.VMEM),
        compiler_params=pltpu.CompilerParams(vmem_limit_bytes=8 << 20),
        cost_estimate=pl.CostEstimate(flops=1 << 23, bytes_accessed=1 << 17, transcendentals=0),
        name="fold",
    )(*[in_vmem(x) for x in args])


def stage_kernel(integrals_ref, occupied_ref, outputs_ref, staged_ref, key_ref, outputs_out, occupied, sems):
    pieces = sems.shape[0] - 2
    size = integrals_ref.shape[0] // pieces
    copies = [
        pltpu.make_async_copy(src, dst, sems.at[n])
        for n, (src, dst) in enumerate(
            ((occupied_ref, occupied), (outputs_ref, outputs_out))
        )
    ]
    for n in range(pieces):
        rows = pl.ds(n * size, size)
        copies.append(pltpu.make_async_copy(integrals_ref.at[rows], staged_ref.at[rows], sems.at[2 + n]))
    for copy in copies:
        copy.start()
    copies[0].wait()
    block = key_ref.shape[0]
    key = keys(occupied[...], lax.axis_index("col"), block)
    lane = lax.broadcasted_iota(jnp.int32, (block, block), 1)
    sublane = lax.broadcasted_iota(jnp.int32, (block, block), 0)
    column = jnp.sum(jnp.where(lane == sublane, key, 0), axis=1, keepdims=True)
    key_ref[...] = jnp.broadcast_to(column, key_ref.shape)
    for copy in copies[1:]:
        copy.wait()


def stage(integrals, occupied_irreps, outputs, block, pieces=4):
    depth, width = integrals.shape
    pairs = occupied_irreps.shape[0]
    return pl.pallas_call(
        stage_kernel,
        out_shape=(
            pltpu.VMEM(integrals.shape, integrals.dtype),
            pltpu.VMEM((block, 128), jnp.int32),
            pltpu.VMEM((1, width), jnp.int32),
        ),
        in_specs=[pl.BlockSpec(memory_space=pltpu.HBM)] * 3,
        out_specs=[pl.BlockSpec(memory_space=pltpu.VMEM)] * 3,
        scratch_shapes=[pltpu.VMEM((1, pairs), jnp.int32), pltpu.SemaphoreType.DMA((2 + pieces,))],
        compiler_params=pltpu.CompilerParams(vmem_limit_bytes=8 << 20),
        cost_estimate=pl.CostEstimate(flops=0, bytes_accessed=4 * integrals.size, transcendentals=0),
        name="stage",
    )(*[in_hbm(x) for x in (integrals, occupied_irreps.reshape(1, pairs), outputs.reshape(1, width))])


def sums_kernel(slots, blocks_refs, contracted_ref, outputs_ref, other_outputs_ref, integrals_ref, other_ref, send_ref, far_ref, keep_ref):
    row, col = lax.axis_index("row"), lax.axis_index("col")
    place, member = row // CORES, row % CORES
    contracted = contracted_ref[...]
    blocks = [ref[...].astype(jnp.float32) for ref in blocks_refs]

    def block(t):
        offset = ((col + t) % COLS) ^ place
        turned = jnp.where((offset == 1) | (offset == 2), offset ^ ((1 - member) * 3), offset)
        chosen = blocks[0]
        for n in range(1, PLACES):
            chosen = jnp.where(turned == n, blocks[n], chosen)
        return chosen

    def product(rows, weights, outputs):
        spread = jnp.concatenate([jnp.where(contracted == g, rows, 0.0) for g in range(IRREPS)], axis=0)
        each = jnp.dot(spread.astype(jnp.bfloat16), weights, preferred_element_type=jnp.float32)
        total = jnp.zeros((2 * slots, each.shape[1]), jnp.float32)
        for g in range(IRREPS):
            total = jnp.where(outputs == g, each[g * 2 * slots : (g + 1) * 2 * slots], total)
        return total

    sent = block(1 + member)
    theirs = product(jnp.concatenate([sent, block(3)], 0), other_ref[...], other_outputs_ref[...])
    send_ref[:slots] = theirs[:slots]
    far_ref[...] = theirs[slots:]
    ours = product(jnp.concatenate([sent, block(0)], 0), integrals_ref[...], outputs_ref[...])
    send_ref[slots:] = ours[:slots]
    keep_ref[...] = ours[slots:]


def sums(blocks, contracted, outputs, other_outputs, integrals, other, slots):
    depth, width = integrals.shape

    def kernel(b0, b1, b2, b3, *refs):
        sums_kernel(slots, (b0, b1, b2, b3), *refs)

    args = [*blocks, contracted.reshape(1, depth), outputs.reshape(1, width), other_outputs.reshape(1, width), integrals, other]
    return pl.pallas_call(
        kernel,
        out_shape=(
            pltpu.VMEM((2 * slots, width), jnp.float32),
            pltpu.VMEM((slots, width), jnp.float32),
            pltpu.VMEM((slots, width), jnp.float32),
        ),
        in_specs=[pl.BlockSpec(memory_space=pltpu.VMEM)] * len(args),
        out_specs=[pl.BlockSpec(memory_space=pltpu.VMEM)] * 3,
        compiler_params=pltpu.CompilerParams(vmem_limit_bytes=16 << 20),
        cost_estimate=pl.CostEstimate(flops=1 << 28, bytes_accessed=1 << 21, transcendentals=0),
        name="sums",
    )(*[in_vmem(x) for x in args])


def expand_kernel(keep_ref, got_ref, far_ref, too_ref, key_ref, outputs_ref, out_ref, staged, sems):
    slots, width = keep_ref.shape
    block = key_ref.shape[0]
    outputs = outputs_ref[...]
    total = (keep_ref[...] + got_ref[:slots]) + (far_ref[...] + too_ref[...])
    pieces = sems.shape[0]
    size = block // pieces
    copies = []
    for n in range(pieces):
        rows = slice(n * size, (n + 1) * size)
        key = key_ref[rows, :1]
        out = jnp.zeros((size, width), jnp.float32)
        for s in range(slots):
            out = jnp.where(key == outputs * slots + s, total[s : s + 1], out)
        staged[rows] = out
        copy = pltpu.make_async_copy(staged.at[rows], out_ref.at[rows], sems.at[n])
        copy.start()
        copies.append(copy)
    for copy in copies:
        copy.wait()


def expand(keep, got, far, too, key, outputs, pieces=2):
    slots, width = keep.shape
    block = key.shape[0]
    args = [keep, got, far, too, key, outputs.reshape(1, width)]
    return pl.pallas_call(
        expand_kernel,
        out_shape=pltpu.HBM((block, width), jnp.float32),
        in_specs=[pl.BlockSpec(memory_space=pltpu.VMEM)] * len(args),
        out_specs=pl.BlockSpec(memory_space=pltpu.HBM),
        scratch_shapes=[pltpu.VMEM((block, width), jnp.float32), pltpu.SemaphoreType.DMA((pieces,))],
        compiler_params=pltpu.CompilerParams(vmem_limit_bytes=8 << 20),
        cost_estimate=pl.CostEstimate(flops=1 << 20, bytes_accessed=1 << 18, transcendentals=0),
        name="expand",
    )(*[in_vmem(x) for x in args])


def move(x, target):
    pairs = []
    for r in range(PLACES * CORES):
        for c in range(COLS):
            place, member, col = target(r // CORES, r % CORES, c)
            pairs.append((r * COLS + c, (place * CORES + member) * COLS + col))
    return lax.ppermute(x, ("row", "col"), pairs)


def quad(amplitudes, integrals, occupied_irreps, contracted_irreps, output_irreps):
    own = amplitudes.shape[0]
    block = own * CORES
    slots = block // IRREPS
    sibling = lambda p, m, c: (p, 1 - m, c)

    raw = move(amplitudes, sibling)
    order, contracted, ours = pack(occupied_irreps, contracted_irreps, amplitudes, block)
    raw, order, late_integrals, late_outputs = lax.optimization_barrier((raw, order, integrals, output_irreps))
    other = move(late_integrals, sibling)
    other_outputs = move(late_outputs, sibling)
    packed = fold(order, contracted, ours, raw, slots)

    packed, late_integrals = lax.optimization_barrier((packed, integrals))
    side = move(packed, lambda p, m, c: (p ^ (1 + m), 1 - m, c))
    far = move(packed, lambda p, m, c: (p ^ 3, 1 - m, c))
    staged, key, outputs = stage(late_integrals, occupied_irreps, output_irreps, block)
    side_too = move(side, sibling)
    send, send_far, keep = sums(
        (packed, side, side_too, far), contracted, outputs, other_outputs, staged, other, slots
    )
    got = move(send, lambda p, m, c: (p, 1 - m, (c + 1 + m) % COLS))
    got_far = move(send_far, lambda p, m, c: (p, 1 - m, (c + 3) % COLS))
    got_too = move(got[slots:], sibling)
    return expand(keep, got, got_far, got_too, key, outputs)


def solution(mesh):
    small = mesh.shape["row"] == PLACES * CORES and mesh.shape["col"] == COLS
    return jax.shard_map(
        quad if small else general,
        mesh=mesh,
        in_specs=(P("row", "col"), P("col", "row"), P(), P("col"), P("row")),
        out_specs=P("col", "row"),
        check_vma=False,
    )
```

```python
import functools

import jax
import jax.numpy as jnp
from jax import lax
from jax.experimental import pallas as pl
from jax.experimental.pallas import tpu as pltpu
from jax.sharding import PartitionSpec as P

IRREPS = 8
CORES, PLACES, COLS = 2, 4, 4
LABEL_ROWS = 16


def in_hbm(x):
    return pltpu.with_memory_space_constraint(x, pltpu.HBM)


def in_vmem(x):
    return pltpu.with_memory_space_constraint(x, pltpu.VMEM)


def swap(x, axis, mask):
    count = lax.axis_size(axis)
    return lax.ppermute(x, axis, [(i, i ^ mask) for i in range(count)])


def ranks(labels, order):
    same = labels[:, None] == labels[None, :]
    before = order[None, :] < order[:, None]
    return jnp.sum((same & before).astype(jnp.int32), axis=1)


def general(amplitudes, integrals, occupied_irreps, contracted_irreps, output_irreps):
    rows, cols = lax.axis_size("row"), lax.axis_size("col")
    pairs = occupied_irreps.shape[0]
    own = amplitudes.shape[0]
    block = pairs // cols
    slots = block // IRREPS
    share = block // own
    row, col = lax.axis_index("row"), lax.axis_index("col")
    place, member = row // share, row % share

    raw, labels, order = [amplitudes], [], []
    step = 1
    while step < share:
        raw.append(swap(jnp.concatenate(raw, 0), "row", step))
        step *= 2
    raw = jnp.concatenate(raw, 0)
    for j in range(share):
        first = (member ^ j) * own
        labels.append(lax.dynamic_slice_in_dim(occupied_irreps, place * block + first, own, 0))
        order.append(first + jnp.arange(own, dtype=jnp.int32))
    labels, order = jnp.concatenate(labels), jnp.concatenate(order)
    rank = ranks(labels, order)
    pick = (rank[None, :] == jnp.arange(slots, dtype=jnp.int32)[:, None]).astype(jnp.bfloat16)
    kept = jnp.where(labels[:, None] == contracted_irreps[None, :], raw, jnp.zeros_like(raw))
    packed = jnp.dot(pick, kept, preferred_element_type=jnp.float32).astype(jnp.bfloat16)

    step = share
    while step < rows:
        packed = jnp.concatenate([packed, swap(packed, "row", step)], 0)
        step *= 2
    masked = jnp.where(contracted_irreps[:, None] == output_irreps[None, :], integrals, jnp.zeros_like(integrals))
    sums = jnp.dot(packed, masked, preferred_element_type=jnp.float32)
    turn = col ^ place
    parts = [lax.dynamic_slice_in_dim(sums, (turn ^ t) * slots, slots, 0) for t in range(cols)]
    step = 1
    while step < cols:
        got = swap(jnp.concatenate(parts[1::2], 0), "col", step)
        parts = [part + got[t * slots : (t + 1) * slots] for t, part in enumerate(parts[::2])]
        step *= 2
    total = parts[0]

    mine = lax.dynamic_slice_in_dim(occupied_irreps, col * block, block, 0)
    slot = ranks(mine, jnp.arange(block, dtype=jnp.int32))
    out = jnp.zeros((block, total.shape[1]), jnp.float32)
    match = mine[:, None] == output_irreps[None, :]
    for s in range(slots):
        out = jnp.where(match & (slot[:, None] == s), total[s][None, :], out)
    return out


def keys(occupied, place, block):
    slots = block // IRREPS
    labels = jnp.zeros((1, block), jnp.int32)
    for b in range(occupied.shape[1] // block):
        labels = jnp.where(place == b, occupied[:, b * block : (b + 1) * block], labels)
    irrep = lax.broadcasted_iota(jnp.int32, (IRREPS, block), 0)
    same = jnp.where(labels == irrep, 1.0, 0.0)
    lane = lax.broadcasted_iota(jnp.int32, (block, block), 1)
    sublane = lax.broadcasted_iota(jnp.int32, (block, block), 0)
    before = jnp.where(sublane < lane, 1.0, 0.0).astype(jnp.bfloat16)
    counts = jnp.dot(same.astype(jnp.bfloat16), before, preferred_element_type=jnp.float32)
    rank = jnp.sum(same * counts, axis=0, keepdims=True)
    return labels * slots + rank.astype(jnp.int32)


def pack_kernel(block, occupied_ref, contracted_ref, outputs_ref, amplitudes_ref, integrals_ref, order_ref, key_ref, contracted_out, outputs_out, own_out, staged_ref, occupied, sems):
    copies = [
        pltpu.make_async_copy(src, dst, sems.at[n])
        for n, (src, dst) in enumerate(
            (
                (occupied_ref, occupied),
                (contracted_ref, contracted_out),
                (outputs_ref, outputs_out),
                (amplitudes_ref, own_out),
                (integrals_ref, staged_ref.at[pl.ds(0, integrals_ref.shape[0])]),
            )
        )
    ]
    for copy in copies:
        copy.start()
    copies[0].wait()
    key = keys(occupied[...], lax.axis_index("row") // CORES, block)
    sublane = lax.broadcasted_iota(jnp.int32, (block, block), 0)
    order_ref[...] = jnp.where(key == sublane, 1.0, 0.0).astype(jnp.bfloat16)
    key = keys(occupied[...], lax.axis_index("col"), block)
    lane = lax.broadcasted_iota(jnp.int32, (block, block), 1)
    column = jnp.sum(jnp.where(lane == sublane, key, 0), axis=1, keepdims=True)
    key_ref[...] = jnp.broadcast_to(column, key_ref.shape)
    copies[2].wait()
    labels = outputs_out[...].astype(jnp.float32).astype(jnp.bfloat16)
    staged_ref[integrals_ref.shape[0] :] = jnp.broadcast_to(labels, (LABEL_ROWS, labels.shape[1]))
    for copy in (copies[1], *copies[3:]):
        copy.wait()


def pack(occupied_irreps, contracted_irreps, output_irreps, amplitudes, integrals, block):
    rows, depth = amplitudes.shape
    width = output_irreps.shape[0]
    pairs = occupied_irreps.shape[0]
    args = (
        occupied_irreps.reshape(1, pairs),
        contracted_irreps.reshape(1, depth),
        output_irreps.reshape(1, width),
        amplitudes,
        integrals,
    )
    return pl.pallas_call(
        functools.partial(pack_kernel, block),
        out_shape=(
            pltpu.VMEM((block, block), jnp.bfloat16),
            pltpu.VMEM((block, 128), jnp.int32),
            pltpu.VMEM((1, depth), jnp.int32),
            pltpu.VMEM((1, width), jnp.int32),
            pltpu.VMEM((rows, depth), jnp.bfloat16),
            pltpu.VMEM((depth + LABEL_ROWS, width), jnp.bfloat16),
        ),
        in_specs=[pl.BlockSpec(memory_space=pltpu.HBM)] * len(args),
        out_specs=[pl.BlockSpec(memory_space=pltpu.VMEM)] * 6,
        scratch_shapes=[pltpu.VMEM((1, pairs), jnp.int32), pltpu.SemaphoreType.DMA((len(args),))],
        compiler_params=pltpu.CompilerParams(vmem_limit_bytes=8 << 20),
        cost_estimate=pl.CostEstimate(flops=1 << 20, bytes_accessed=1 << 18, transcendentals=0),
        name="pack",
    )(*[in_hbm(x) for x in args])


def fold_kernel(slots, order_ref, contracted_ref, own_ref, raw_ref, packed_ref):
    first = lax.axis_index("row") % CORES == 0
    own, raw = own_ref[...], raw_ref[...]
    rows = jnp.concatenate([jnp.where(first, own, raw), jnp.where(first, raw, own)], axis=0)
    ordered = jnp.dot(order_ref[...], rows, preferred_element_type=jnp.float32)
    contracted = contracted_ref[...]
    packed = jnp.zeros((slots, contracted.shape[1]), jnp.float32)
    for g in range(IRREPS):
        packed = jnp.where(contracted == g, ordered[g * slots : (g + 1) * slots], packed)
    packed_ref[...] = packed.astype(jnp.bfloat16)


def fold(order, contracted, own, raw, slots):
    args = [order, contracted, own, raw]
    return pl.pallas_call(
        functools.partial(fold_kernel, slots),
        out_shape=pltpu.VMEM((slots, own.shape[1]), jnp.bfloat16),
        in_specs=[pl.BlockSpec(memory_space=pltpu.VMEM)] * len(args),
        out_specs=pl.BlockSpec(memory_space=pltpu.VMEM),
        compiler_params=pltpu.CompilerParams(vmem_limit_bytes=8 << 20),
        cost_estimate=pl.CostEstimate(flops=1 << 23, bytes_accessed=1 << 17, transcendentals=0),
        name="fold",
    )(*[in_vmem(x) for x in args])


def sums_kernel(slots, blocks_refs, contracted_ref, staged_ref, other_ref, send_ref, far_ref, keep_ref):
    row, col = lax.axis_index("row"), lax.axis_index("col")
    place, member = row // CORES, row % CORES
    contracted = contracted_ref[...]
    blocks = [ref[...].astype(jnp.float32) for ref in blocks_refs]

    def block(t):
        back = (place - col - t) % PLACES
        turned = jnp.where((back == 1) | (back == 2), 1 + (back + member) % 2, back)
        chosen = blocks[0]
        for n in range(1, PLACES):
            chosen = jnp.where(turned == n, blocks[n], chosen)
        return chosen

    depth = contracted.shape[1]

    def product(rows, ref):
        outputs = ref[depth : depth + 1].astype(jnp.float32)
        spread = jnp.concatenate([jnp.where(contracted == g, rows, 0.0) for g in range(IRREPS)], axis=0)
        each = jnp.dot(spread.astype(jnp.bfloat16), ref[:depth], preferred_element_type=jnp.float32)
        total = jnp.zeros((2 * slots, each.shape[1]), jnp.float32)
        for g in range(IRREPS):
            total = jnp.where(outputs == g, each[g * 2 * slots : (g + 1) * 2 * slots], total)
        return total

    sent = block(1 + member)
    theirs = product(jnp.concatenate([sent, block(3)], 0), other_ref)
    send_ref[:slots] = theirs[:slots]
    far_ref[...] = theirs[slots:]
    ours = product(jnp.concatenate([sent, block(0)], 0), staged_ref)
    send_ref[slots:] = ours[:slots]
    keep_ref[...] = ours[slots:]


def sums(blocks, contracted, staged, other, slots):
    width = staged.shape[1]

    def kernel(b0, b1, b2, b3, *refs):
        sums_kernel(slots, (b0, b1, b2, b3), *refs)

    args = [*blocks, contracted, staged, other]
    return pl.pallas_call(
        kernel,
        out_shape=(
            pltpu.VMEM((2 * slots, width), jnp.float32),
            pltpu.VMEM((slots, width), jnp.float32),
            pltpu.VMEM((slots, width), jnp.float32),
        ),
        in_specs=[pl.BlockSpec(memory_space=pltpu.VMEM)] * len(args),
        out_specs=[pl.BlockSpec(memory_space=pltpu.VMEM)] * 3,
        compiler_params=pltpu.CompilerParams(vmem_limit_bytes=16 << 20),
        cost_estimate=pl.CostEstimate(flops=1 << 28, bytes_accessed=1 << 21, transcendentals=0),
        name="sums",
    )(*[in_vmem(x) for x in args])


def expand_kernel(keep_ref, got_ref, far_ref, too_ref, key_ref, outputs_ref, out_ref, staged, sems):
    slots, width = keep_ref.shape
    block = key_ref.shape[0]
    outputs = outputs_ref[...]
    total = (keep_ref[...] + got_ref[:slots]) + (far_ref[...] + too_ref[...])
    pieces = sems.shape[0]
    size = block // pieces
    copies = []
    for n in range(pieces):
        rows = slice(n * size, (n + 1) * size)
        key = key_ref[rows, :1]
        out = jnp.zeros((size, width), jnp.float32)
        for s in range(slots):
            out = jnp.where(key == outputs * slots + s, total[s : s + 1], out)
        staged[rows] = out
        copy = pltpu.make_async_copy(staged.at[rows], out_ref.at[rows], sems.at[n])
        copy.start()
        copies.append(copy)
    for copy in copies:
        copy.wait()


def expand(keep, got, far, too, key, outputs, pieces=2):
    slots, width = keep.shape
    block = key.shape[0]
    args = [keep, got, far, too, key, outputs.reshape(1, width)]
    return pl.pallas_call(
        expand_kernel,
        out_shape=pltpu.HBM((block, width), jnp.float32),
        in_specs=[pl.BlockSpec(memory_space=pltpu.VMEM)] * len(args),
        out_specs=pl.BlockSpec(memory_space=pltpu.HBM),
        scratch_shapes=[pltpu.VMEM((block, width), jnp.float32), pltpu.SemaphoreType.DMA((pieces,))],
        compiler_params=pltpu.CompilerParams(vmem_limit_bytes=8 << 20),
        cost_estimate=pl.CostEstimate(flops=1 << 20, bytes_accessed=1 << 18, transcendentals=0),
        name="expand",
    )(*[in_vmem(x) for x in args])


def move(x, target):
    pairs = []
    for r in range(PLACES * CORES):
        for c in range(COLS):
            place, member, col = target(r // CORES, r % CORES, c)
            pairs.append((r * COLS + c, (place * CORES + member) * COLS + col))
    return lax.ppermute(x, ("row", "col"), pairs)


def quad(amplitudes, integrals, occupied_irreps, contracted_irreps, output_irreps):
    own = amplitudes.shape[0]
    block = own * CORES
    slots = block // IRREPS
    sibling = lambda p, m, c: (p, 1 - m, c)

    raw = move(amplitudes, sibling)
    order, key, contracted, outputs, ours, staged = pack(
        occupied_irreps, contracted_irreps, output_irreps, amplitudes, integrals, block
    )
    raw, order, staged = lax.optimization_barrier((raw, order, staged))
    other = move(staged, sibling)
    packed = fold(order, contracted, ours, raw, slots)

    side = move(packed, lambda p, m, c: ((p + 1 + m) % PLACES, 1 - m, c))
    far = move(packed, lambda p, m, c: ((p + 3) % PLACES, 1 - m, c))
    side_too = move(side, sibling)
    send, send_far, keep = sums(
        (packed, side, side_too, far), contracted, staged, other, slots
    )
    got = move(send, lambda p, m, c: (p, 1 - m, (c + 1 + m) % COLS))
    got_far = move(send_far, lambda p, m, c: (p, 1 - m, (c + 3) % COLS))
    got_too = move(got[slots:], sibling)
    return expand(keep, got, got_far, got_too, key, outputs)


def solution(mesh):
    small = mesh.shape["row"] == PLACES * CORES and mesh.shape["col"] == COLS
    return jax.shard_map(
        quad if small else general,
        mesh=mesh,
        in_specs=(P("row", "col"), P("col", "row"), P(), P("col"), P("row")),
        out_specs=P("col", "row"),
        check_vma=False,
    )
```

```python
import functools

import jax
import jax.numpy as jnp
from jax import lax
from jax.experimental import pallas as pl
from jax.experimental.pallas import tpu as pltpu
from jax.sharding import PartitionSpec as P

IRREPS = 8
CORES, PLACES, COLS = 2, 4, 4
LABEL_ROWS = 16


def in_hbm(x):
    return pltpu.with_memory_space_constraint(x, pltpu.HBM)


def in_vmem(x):
    return pltpu.with_memory_space_constraint(x, pltpu.VMEM)


def swap(x, axis, mask):
    count = lax.axis_size(axis)
    return lax.ppermute(x, axis, [(i, i ^ mask) for i in range(count)])


def ranks(labels, order):
    same = labels[:, None] == labels[None, :]
    before = order[None, :] < order[:, None]
    return jnp.sum((same & before).astype(jnp.int32), axis=1)


def general(amplitudes, integrals, occupied_irreps, contracted_irreps, output_irreps):
    rows, cols = lax.axis_size("row"), lax.axis_size("col")
    pairs = occupied_irreps.shape[0]
    own = amplitudes.shape[0]
    block = pairs // cols
    slots = block // IRREPS
    share = block // own
    row, col = lax.axis_index("row"), lax.axis_index("col")
    place, member = row // share, row % share

    raw, labels, order = [amplitudes], [], []
    step = 1
    while step < share:
        raw.append(swap(jnp.concatenate(raw, 0), "row", step))
        step *= 2
    raw = jnp.concatenate(raw, 0)
    for j in range(share):
        first = (member ^ j) * own
        labels.append(lax.dynamic_slice_in_dim(occupied_irreps, place * block + first, own, 0))
        order.append(first + jnp.arange(own, dtype=jnp.int32))
    labels, order = jnp.concatenate(labels), jnp.concatenate(order)
    rank = ranks(labels, order)
    pick = (rank[None, :] == jnp.arange(slots, dtype=jnp.int32)[:, None]).astype(jnp.bfloat16)
    kept = jnp.where(labels[:, None] == contracted_irreps[None, :], raw, jnp.zeros_like(raw))
    packed = jnp.dot(pick, kept, preferred_element_type=jnp.float32).astype(jnp.bfloat16)

    step = share
    while step < rows:
        packed = jnp.concatenate([packed, swap(packed, "row", step)], 0)
        step *= 2
    masked = jnp.where(contracted_irreps[:, None] == output_irreps[None, :], integrals, jnp.zeros_like(integrals))
    sums = jnp.dot(packed, masked, preferred_element_type=jnp.float32)
    turn = col ^ place
    parts = [lax.dynamic_slice_in_dim(sums, (turn ^ t) * slots, slots, 0) for t in range(cols)]
    step = 1
    while step < cols:
        got = swap(jnp.concatenate(parts[1::2], 0), "col", step)
        parts = [part + got[t * slots : (t + 1) * slots] for t, part in enumerate(parts[::2])]
        step *= 2
    total = parts[0]

    mine = lax.dynamic_slice_in_dim(occupied_irreps, col * block, block, 0)
    slot = ranks(mine, jnp.arange(block, dtype=jnp.int32))
    out = jnp.zeros((block, total.shape[1]), jnp.float32)
    match = mine[:, None] == output_irreps[None, :]
    for s in range(slots):
        out = jnp.where(match & (slot[:, None] == s), total[s][None, :], out)
    return out


def keys(occupied, place, block):
    slots = block // IRREPS
    labels = jnp.zeros((1, block), jnp.int32)
    for b in range(occupied.shape[1] // block):
        labels = jnp.where(place == b, occupied[:, b * block : (b + 1) * block], labels)
    irrep = lax.broadcasted_iota(jnp.int32, (IRREPS, block), 0)
    same = jnp.where(labels == irrep, 1.0, 0.0)
    lane = lax.broadcasted_iota(jnp.int32, (block, block), 1)
    sublane = lax.broadcasted_iota(jnp.int32, (block, block), 0)
    before = jnp.where(sublane < lane, 1.0, 0.0).astype(jnp.bfloat16)
    counts = jnp.dot(same.astype(jnp.bfloat16), before, preferred_element_type=jnp.float32)
    rank = jnp.sum(same * counts, axis=0, keepdims=True)
    return labels * slots + rank.astype(jnp.int32)


def pack_kernel(block, occupied_ref, contracted_ref, outputs_ref, amplitudes_ref, integrals_ref, order_ref, key_ref, contracted_out, outputs_out, own_out, staged_ref, occupied, sems):
    copies = [
        pltpu.make_async_copy(src, dst, sems.at[n])
        for n, (src, dst) in enumerate(
            (
                (occupied_ref, occupied),
                (contracted_ref, contracted_out),
                (outputs_ref, outputs_out),
                (amplitudes_ref, own_out),
                (integrals_ref, staged_ref.at[pl.ds(0, integrals_ref.shape[0])]),
            )
        )
    ]
    for copy in copies:
        copy.start()
    copies[0].wait()
    key = keys(occupied[...], lax.axis_index("row") // CORES, block)
    sublane = lax.broadcasted_iota(jnp.int32, (block, block), 0)
    order_ref[...] = jnp.where(key == sublane, 1.0, 0.0).astype(jnp.bfloat16)
    key = keys(occupied[...], lax.axis_index("col"), block)
    lane = lax.broadcasted_iota(jnp.int32, (block, block), 1)
    column = jnp.sum(jnp.where(lane == sublane, key, 0), axis=1, keepdims=True)
    key_ref[...] = jnp.broadcast_to(column, key_ref.shape)
    copies[2].wait()
    labels = outputs_out[...].astype(jnp.float32).astype(jnp.bfloat16)
    staged_ref[integrals_ref.shape[0] :] = jnp.broadcast_to(labels, (LABEL_ROWS, labels.shape[1]))
    for copy in (copies[1], *copies[3:]):
        copy.wait()


def pack(occupied_irreps, contracted_irreps, output_irreps, amplitudes, integrals, block):
    rows, depth = amplitudes.shape
    width = output_irreps.shape[0]
    pairs = occupied_irreps.shape[0]
    args = (
        occupied_irreps.reshape(1, pairs),
        contracted_irreps.reshape(1, depth),
        output_irreps.reshape(1, width),
        amplitudes,
        integrals,
    )
    return pl.pallas_call(
        functools.partial(pack_kernel, block),
        out_shape=(
            pltpu.VMEM((block, block), jnp.bfloat16),
            pltpu.VMEM((block, 128), jnp.int32),
            pltpu.VMEM((1, depth), jnp.int32),
            pltpu.VMEM((1, width), jnp.int32),
            pltpu.VMEM((rows, depth), jnp.bfloat16),
            pltpu.VMEM((depth + LABEL_ROWS, width), jnp.bfloat16),
        ),
        in_specs=[pl.BlockSpec(memory_space=pltpu.HBM)] * len(args),
        out_specs=[pl.BlockSpec(memory_space=pltpu.VMEM)] * 6,
        scratch_shapes=[pltpu.VMEM((1, pairs), jnp.int32), pltpu.SemaphoreType.DMA((len(args),))],
        compiler_params=pltpu.CompilerParams(vmem_limit_bytes=8 << 20),
        cost_estimate=pl.CostEstimate(flops=1 << 20, bytes_accessed=1 << 18, transcendentals=0),
        name="pack",
    )(*[in_hbm(x) for x in args])


def fold_kernel(slots, order_ref, contracted_ref, own_ref, raw_ref, packed_ref):
    first = lax.axis_index("row") % CORES == 0
    own, raw = own_ref[...], raw_ref[...]
    rows = jnp.concatenate([jnp.where(first, own, raw), jnp.where(first, raw, own)], axis=0)
    ordered = jnp.dot(order_ref[...], rows, preferred_element_type=jnp.float32)
    contracted = contracted_ref[...]
    packed = jnp.zeros((slots, contracted.shape[1]), jnp.float32)
    for g in range(IRREPS):
        packed = jnp.where(contracted == g, ordered[g * slots : (g + 1) * slots], packed)
    packed_ref[...] = packed.astype(jnp.bfloat16)


def fold(order, contracted, own, raw, slots):
    args = [order, contracted, own, raw]
    return pl.pallas_call(
        functools.partial(fold_kernel, slots),
        out_shape=pltpu.VMEM((slots, own.shape[1]), jnp.bfloat16),
        in_specs=[pl.BlockSpec(memory_space=pltpu.VMEM)] * len(args),
        out_specs=pl.BlockSpec(memory_space=pltpu.VMEM),
        compiler_params=pltpu.CompilerParams(vmem_limit_bytes=8 << 20),
        cost_estimate=pl.CostEstimate(flops=1 << 23, bytes_accessed=1 << 17, transcendentals=0),
        name="fold",
    )(*[in_vmem(x) for x in args])


def sums_kernel(slots, blocks_refs, contracted_ref, staged_ref, other_ref, send_ref, far_ref, keep_ref):
    row, col = lax.axis_index("row"), lax.axis_index("col")
    place, member = row // CORES, row % CORES
    contracted = contracted_ref[...]
    blocks = [ref[...].astype(jnp.float32) for ref in blocks_refs]

    def block(t):
        back = (place - col - t) % PLACES
        turned = jnp.where((back == 1) | (back == 2), 1 + (back + member) % 2, back)
        chosen = blocks[0]
        for n in range(1, PLACES):
            chosen = jnp.where(turned == n, blocks[n], chosen)
        return chosen

    depth = contracted.shape[1]

    def product(rows, ref):
        outputs = ref[depth : depth + 1].astype(jnp.float32)
        spread = jnp.concatenate([jnp.where(contracted == g, rows, 0.0) for g in range(IRREPS)], axis=0)
        each = jnp.dot(spread.astype(jnp.bfloat16), ref[:depth], preferred_element_type=jnp.float32)
        total = jnp.zeros((2 * slots, each.shape[1]), jnp.float32)
        for g in range(IRREPS):
            total = jnp.where(outputs == g, each[g * 2 * slots : (g + 1) * 2 * slots], total)
        return total

    sent = block(2 - member)
    theirs = product(jnp.concatenate([sent, block(3)], 0), other_ref)
    send_ref[slots:] = theirs[:slots]
    far_ref[...] = theirs[slots:]
    ours = product(jnp.concatenate([sent, block(0)], 0), staged_ref)
    send_ref[:slots] = ours[:slots]
    keep_ref[...] = ours[slots:]


def sums(blocks, contracted, staged, other, slots):
    width = staged.shape[1]

    def kernel(b0, b1, b2, b3, *refs):
        sums_kernel(slots, (b0, b1, b2, b3), *refs)

    args = [*blocks, contracted, staged, other]
    return pl.pallas_call(
        kernel,
        out_shape=(
            pltpu.VMEM((2 * slots, width), jnp.float32),
            pltpu.VMEM((slots, width), jnp.float32),
            pltpu.VMEM((slots, width), jnp.float32),
        ),
        in_specs=[pl.BlockSpec(memory_space=pltpu.VMEM)] * len(args),
        out_specs=[pl.BlockSpec(memory_space=pltpu.VMEM)] * 3,
        compiler_params=pltpu.CompilerParams(vmem_limit_bytes=16 << 20),
        cost_estimate=pl.CostEstimate(flops=1 << 28, bytes_accessed=1 << 21, transcendentals=0),
        name="sums",
    )(*[in_vmem(x) for x in args])


def expand_kernel(keep_ref, got_ref, far_ref, too_ref, key_ref, outputs_ref, out_ref, staged, sems):
    slots, width = keep_ref.shape
    block = key_ref.shape[0]
    outputs = outputs_ref[...]
    total = (keep_ref[...] + got_ref[:slots]) + (far_ref[...] + too_ref[...])
    pieces = sems.shape[0]
    size = block // pieces
    copies = []
    for n in range(pieces):
        rows = slice(n * size, (n + 1) * size)
        key = key_ref[rows, :1]
        out = jnp.zeros((size, width), jnp.float32)
        for s in range(slots):
            out = jnp.where(key == outputs * slots + s, total[s : s + 1], out)
        staged[rows] = out
        copy = pltpu.make_async_copy(staged.at[rows], out_ref.at[rows], sems.at[n])
        copy.start()
        copies.append(copy)
    for copy in copies:
        copy.wait()


def expand(keep, got, far, too, key, outputs, pieces=2):
    slots, width = keep.shape
    block = key.shape[0]
    args = [keep, got, far, too, key, outputs.reshape(1, width)]
    return pl.pallas_call(
        expand_kernel,
        out_shape=pltpu.HBM((block, width), jnp.float32),
        in_specs=[pl.BlockSpec(memory_space=pltpu.VMEM)] * len(args),
        out_specs=pl.BlockSpec(memory_space=pltpu.HBM),
        scratch_shapes=[pltpu.VMEM((block, width), jnp.float32), pltpu.SemaphoreType.DMA((pieces,))],
        compiler_params=pltpu.CompilerParams(vmem_limit_bytes=8 << 20),
        cost_estimate=pl.CostEstimate(flops=1 << 20, bytes_accessed=1 << 18, transcendentals=0),
        name="expand",
    )(*[in_vmem(x) for x in args])


def move(x, target):
    pairs = []
    for r in range(PLACES * CORES):
        for c in range(COLS):
            place, member, col = target(r // CORES, r % CORES, c)
            pairs.append((r * COLS + c, (place * CORES + member) * COLS + col))
    return lax.ppermute(x, ("row", "col"), pairs)


def quad(amplitudes, integrals, occupied_irreps, contracted_irreps, output_irreps):
    own = amplitudes.shape[0]
    block = own * CORES
    slots = block // IRREPS
    sibling = lambda p, m, c: (p, 1 - m, c)

    raw = move(amplitudes, sibling)
    order, key, contracted, outputs, ours, staged = pack(
        occupied_irreps, contracted_irreps, output_irreps, amplitudes, integrals, block
    )
    raw, order, staged = lax.optimization_barrier((raw, order, staged))
    other = move(staged, sibling)
    packed = fold(order, contracted, ours, raw, slots)

    side = move(packed, lambda p, m, c: ((p + 1 + m) % PLACES, 1 - m, c))
    far = move(packed, lambda p, m, c: ((p + 3) % PLACES, 1 - m, c))
    side_too = move(side, sibling)
    send, send_far, keep = sums(
        (packed, side, side_too, far), contracted, staged, other, slots
    )
    got = move(send, lambda p, m, c: (p, m, (c + 2 - m) % COLS))
    got_far = move(send_far, lambda p, m, c: (p, 1 - m, (c + 3) % COLS))
    got_too = move(got[slots:], sibling)
    return expand(keep, got, got_far, got_too, key, outputs)


def solution(mesh):
    small = mesh.shape["row"] == PLACES * CORES and mesh.shape["col"] == COLS
    return jax.shard_map(
        quad if small else general,
        mesh=mesh,
        in_specs=(P("row", "col"), P("col", "row"), P(), P("col"), P("row")),
        out_specs=P("col", "row"),
        check_vma=False,
    )
```

```python
import functools

import jax
import jax.numpy as jnp
from jax import lax
from jax.experimental import pallas as pl
from jax.experimental.pallas import tpu as pltpu
from jax.sharding import PartitionSpec as P

IRREPS = 8
CORES, PLACES, COLS = 2, 4, 4
LABEL_ROWS = 16


def in_hbm(x):
    return pltpu.with_memory_space_constraint(x, pltpu.HBM)


def in_vmem(x):
    return pltpu.with_memory_space_constraint(x, pltpu.VMEM)


def swap(x, axis, mask):
    count = lax.axis_size(axis)
    return lax.ppermute(x, axis, [(i, i ^ mask) for i in range(count)])


def ranks(labels, order):
    same = labels[:, None] == labels[None, :]
    before = order[None, :] < order[:, None]
    return jnp.sum((same & before).astype(jnp.int32), axis=1)


def general(amplitudes, integrals, occupied_irreps, contracted_irreps, output_irreps):
    rows, cols = lax.axis_size("row"), lax.axis_size("col")
    pairs = occupied_irreps.shape[0]
    own = amplitudes.shape[0]
    block = pairs // cols
    slots = block // IRREPS
    share = block // own
    row, col = lax.axis_index("row"), lax.axis_index("col")
    place, member = row // share, row % share

    raw, labels, order = [amplitudes], [], []
    step = 1
    while step < share:
        raw.append(swap(jnp.concatenate(raw, 0), "row", step))
        step *= 2
    raw = jnp.concatenate(raw, 0)
    for j in range(share):
        first = (member ^ j) * own
        labels.append(lax.dynamic_slice_in_dim(occupied_irreps, place * block + first, own, 0))
        order.append(first + jnp.arange(own, dtype=jnp.int32))
    labels, order = jnp.concatenate(labels), jnp.concatenate(order)
    rank = ranks(labels, order)
    pick = (rank[None, :] == jnp.arange(slots, dtype=jnp.int32)[:, None]).astype(jnp.bfloat16)
    kept = jnp.where(labels[:, None] == contracted_irreps[None, :], raw, jnp.zeros_like(raw))
    packed = jnp.dot(pick, kept, preferred_element_type=jnp.float32).astype(jnp.bfloat16)

    step = share
    while step < rows:
        packed = jnp.concatenate([packed, swap(packed, "row", step)], 0)
        step *= 2
    masked = jnp.where(contracted_irreps[:, None] == output_irreps[None, :], integrals, jnp.zeros_like(integrals))
    sums = jnp.dot(packed, masked, preferred_element_type=jnp.float32)
    turn = col ^ place
    parts = [lax.dynamic_slice_in_dim(sums, (turn ^ t) * slots, slots, 0) for t in range(cols)]
    step = 1
    while step < cols:
        got = swap(jnp.concatenate(parts[1::2], 0), "col", step)
        parts = [part + got[t * slots : (t + 1) * slots] for t, part in enumerate(parts[::2])]
        step *= 2
    total = parts[0]

    mine = lax.dynamic_slice_in_dim(occupied_irreps, col * block, block, 0)
    slot = ranks(mine, jnp.arange(block, dtype=jnp.int32))
    out = jnp.zeros((block, total.shape[1]), jnp.float32)
    match = mine[:, None] == output_irreps[None, :]
    for s in range(slots):
        out = jnp.where(match & (slot[:, None] == s), total[s][None, :], out)
    return out


def keys(occupied, place, block):
    slots = block // IRREPS
    labels = jnp.zeros((1, block), jnp.int32)
    for b in range(occupied.shape[1] // block):
        labels = jnp.where(place == b, occupied[:, b * block : (b + 1) * block], labels)
    irrep = lax.broadcasted_iota(jnp.int32, (IRREPS, block), 0)
    same = jnp.where(labels == irrep, 1.0, 0.0)
    lane = lax.broadcasted_iota(jnp.int32, (block, block), 1)
    sublane = lax.broadcasted_iota(jnp.int32, (block, block), 0)
    before = jnp.where(sublane < lane, 1.0, 0.0).astype(jnp.bfloat16)
    counts = jnp.dot(same.astype(jnp.bfloat16), before, preferred_element_type=jnp.float32)
    rank = jnp.sum(same * counts, axis=0, keepdims=True)
    return labels * slots + rank.astype(jnp.int32)


def pack_kernel(block, occupied_ref, contracted_ref, outputs_ref, amplitudes_ref, integrals_ref, order_ref, key_ref, contracted_out, outputs_out, own_out, staged_ref, occupied, sems):
    copies = [
        pltpu.make_async_copy(src, dst, sems.at[n])
        for n, (src, dst) in enumerate(
            (
                (occupied_ref, occupied),
                (contracted_ref, contracted_out),
                (outputs_ref, outputs_out),
                (amplitudes_ref, own_out),
                (integrals_ref, staged_ref.at[pl.ds(0, integrals_ref.shape[0])]),
            )
        )
    ]
    for copy in copies:
        copy.start()
    copies[0].wait()
    key = keys(occupied[...], lax.axis_index("row") // CORES, block)
    sublane = lax.broadcasted_iota(jnp.int32, (block, block), 0)
    order_ref[...] = jnp.where(key == sublane, 1.0, 0.0).astype(jnp.bfloat16)
    key = keys(occupied[...], lax.axis_index("col"), block)
    lane = lax.broadcasted_iota(jnp.int32, (block, block), 1)
    column = jnp.sum(jnp.where(lane == sublane, key, 0), axis=1, keepdims=True)
    key_ref[...] = jnp.broadcast_to(column, key_ref.shape)
    copies[2].wait()
    labels = outputs_out[...].astype(jnp.float32).astype(jnp.bfloat16)
    staged_ref[integrals_ref.shape[0] :] = jnp.broadcast_to(labels, (LABEL_ROWS, labels.shape[1]))
    for copy in (copies[1], *copies[3:]):
        copy.wait()


def pack(occupied_irreps, contracted_irreps, output_irreps, amplitudes, integrals, block):
    rows, depth = amplitudes.shape
    width = output_irreps.shape[0]
    pairs = occupied_irreps.shape[0]
    args = (
        occupied_irreps.reshape(1, pairs),
        contracted_irreps.reshape(1, depth),
        output_irreps.reshape(1, width),
        amplitudes,
        integrals,
    )
    return pl.pallas_call(
        functools.partial(pack_kernel, block),
        out_shape=(
            pltpu.VMEM((block, block), jnp.bfloat16),
            pltpu.VMEM((block, 128), jnp.int32),
            pltpu.VMEM((1, depth), jnp.int32),
            pltpu.VMEM((1, width), jnp.int32),
            pltpu.VMEM((rows, depth), jnp.bfloat16),
            pltpu.VMEM((depth + LABEL_ROWS, width), jnp.bfloat16),
        ),
        in_specs=[pl.BlockSpec(memory_space=pltpu.HBM)] * len(args),
        out_specs=[pl.BlockSpec(memory_space=pltpu.VMEM)] * 6,
        scratch_shapes=[pltpu.VMEM((1, pairs), jnp.int32), pltpu.SemaphoreType.DMA((len(args),))],
        compiler_params=pltpu.CompilerParams(vmem_limit_bytes=8 << 20),
        cost_estimate=pl.CostEstimate(flops=1 << 20, bytes_accessed=1 << 18, transcendentals=0),
        name="pack",
    )(*[in_hbm(x) for x in args])


def fold_kernel(slots, order_ref, contracted_ref, own_ref, raw_ref, packed_ref):
    first = lax.axis_index("row") % CORES == 0
    own, raw = own_ref[...], raw_ref[...]
    rows = jnp.concatenate([jnp.where(first, own, raw), jnp.where(first, raw, own)], axis=0)
    ordered = jnp.dot(order_ref[...], rows, preferred_element_type=jnp.float32)
    contracted = contracted_ref[...]
    packed = jnp.zeros((slots, contracted.shape[1]), jnp.float32)
    for g in range(IRREPS):
        packed = jnp.where(contracted == g, ordered[g * slots : (g + 1) * slots], packed)
    packed_ref[...] = packed.astype(jnp.bfloat16)


def fold(order, contracted, own, raw, slots):
    args = [order, contracted, own, raw]
    return pl.pallas_call(
        functools.partial(fold_kernel, slots),
        out_shape=pltpu.VMEM((slots, own.shape[1]), jnp.bfloat16),
        in_specs=[pl.BlockSpec(memory_space=pltpu.VMEM)] * len(args),
        out_specs=pl.BlockSpec(memory_space=pltpu.VMEM),
        compiler_params=pltpu.CompilerParams(vmem_limit_bytes=8 << 20),
        cost_estimate=pl.CostEstimate(flops=1 << 23, bytes_accessed=1 << 17, transcendentals=0),
        name="fold",
    )(*[in_vmem(x) for x in args])


def mask_kernel(contracted_ref, staged_ref, other_ref, masked_ref, other_masked_ref):
    depth = masked_ref.shape[0]
    size = 128
    lane = lax.broadcasted_iota(jnp.int32, (size, size), 1)
    sublane = lax.broadcasted_iota(jnp.int32, (size, size), 0)
    labels = [ref[depth : depth + 1].astype(jnp.float32) for ref in (staged_ref, other_ref)]
    for n in range(depth // size):
        rows = slice(n * size, (n + 1) * size)
        row = contracted_ref[:, rows].astype(jnp.float32)
        column = jnp.sum(jnp.where(lane == sublane, row, 0.0), axis=1, keepdims=True)
        for label, src, dst in zip(labels, (staged_ref, other_ref), (masked_ref, other_masked_ref)):
            kept = jnp.where(column == label, src[rows].astype(jnp.float32), 0.0)
            dst[rows] = kept.astype(jnp.bfloat16)


def mask(contracted, staged, other):
    depth, width = contracted.shape[1], staged.shape[1]
    return pl.pallas_call(
        mask_kernel,
        out_shape=(pltpu.VMEM((depth, width), jnp.bfloat16),) * 2,
        in_specs=[pl.BlockSpec(memory_space=pltpu.VMEM)] * 3,
        out_specs=[pl.BlockSpec(memory_space=pltpu.VMEM)] * 2,
        compiler_params=pltpu.CompilerParams(vmem_limit_bytes=16 << 20),
        cost_estimate=pl.CostEstimate(flops=1 << 21, bytes_accessed=1 << 22, transcendentals=0),
        name="mask",
    )(*[in_vmem(x) for x in (contracted, staged, other)])


def sums_kernel(slots, blocks_refs, staged_ref, other_ref, send_ref, far_ref, keep_ref):
    row, col = lax.axis_index("row"), lax.axis_index("col")
    place, member = row // CORES, row % CORES
    blocks = [ref[...].astype(jnp.float32) for ref in blocks_refs]

    def block(t):
        back = (place - col - t) % PLACES
        turned = jnp.where((back == 1) | (back == 2), 1 + (back + member) % 2, back)
        chosen = blocks[0]
        for n in range(1, PLACES):
            chosen = jnp.where(turned == n, blocks[n], chosen)
        return chosen

    def product(rows, ref):
        return jnp.dot(rows.astype(jnp.bfloat16), ref[...], preferred_element_type=jnp.float32)

    sent = block(2 - member)
    theirs = product(jnp.concatenate([sent, block(3)], 0), other_ref)
    send_ref[slots:] = theirs[:slots]
    far_ref[...] = theirs[slots:]
    ours = product(jnp.concatenate([sent, block(0)], 0), staged_ref)
    send_ref[:slots] = ours[:slots]
    keep_ref[...] = ours[slots:]


def sums(blocks, staged, other, slots):
    width = staged.shape[1]

    def kernel(b0, b1, b2, b3, *refs):
        sums_kernel(slots, (b0, b1, b2, b3), *refs)

    args = [*blocks, staged, other]
    return pl.pallas_call(
        kernel,
        out_shape=(
            pltpu.VMEM((2 * slots, width), jnp.float32),
            pltpu.VMEM((slots, width), jnp.float32),
            pltpu.VMEM((slots, width), jnp.float32),
        ),
        in_specs=[pl.BlockSpec(memory_space=pltpu.VMEM)] * len(args),
        out_specs=[pl.BlockSpec(memory_space=pltpu.VMEM)] * 3,
        compiler_params=pltpu.CompilerParams(vmem_limit_bytes=16 << 20),
        cost_estimate=pl.CostEstimate(flops=1 << 28, bytes_accessed=1 << 21, transcendentals=0),
        name="sums",
    )(*[in_vmem(x) for x in args])


def expand_kernel(keep_ref, got_ref, far_ref, too_ref, key_ref, outputs_ref, out_ref, staged, sems):
    slots, width = keep_ref.shape
    block = key_ref.shape[0]
    outputs = outputs_ref[...]
    total = (keep_ref[...] + got_ref[:slots]) + (far_ref[...] + too_ref[...])
    pieces = sems.shape[0]
    size = block // pieces
    copies = []
    for n in range(pieces):
        rows = slice(n * size, (n + 1) * size)
        key = key_ref[rows, :1]
        out = jnp.zeros((size, width), jnp.float32)
        for s in range(slots):
            out = jnp.where(key == outputs * slots + s, total[s : s + 1], out)
        staged[rows] = out
        copy = pltpu.make_async_copy(staged.at[rows], out_ref.at[rows], sems.at[n])
        copy.start()
        copies.append(copy)
    for copy in copies:
        copy.wait()


def expand(keep, got, far, too, key, outputs, pieces=2):
    slots, width = keep.shape
    block = key.shape[0]
    args = [keep, got, far, too, key, outputs.reshape(1, width)]
    return pl.pallas_call(
        expand_kernel,
        out_shape=pltpu.HBM((block, width), jnp.float32),
        in_specs=[pl.BlockSpec(memory_space=pltpu.VMEM)] * len(args),
        out_specs=pl.BlockSpec(memory_space=pltpu.HBM),
        scratch_shapes=[pltpu.VMEM((block, width), jnp.float32), pltpu.SemaphoreType.DMA((pieces,))],
        compiler_params=pltpu.CompilerParams(vmem_limit_bytes=8 << 20),
        cost_estimate=pl.CostEstimate(flops=1 << 20, bytes_accessed=1 << 18, transcendentals=0),
        name="expand",
    )(*[in_vmem(x) for x in args])


def move(x, target):
    pairs = []
    for r in range(PLACES * CORES):
        for c in range(COLS):
            place, member, col = target(r // CORES, r % CORES, c)
            pairs.append((r * COLS + c, (place * CORES + member) * COLS + col))
    return lax.ppermute(x, ("row", "col"), pairs)


def quad(amplitudes, integrals, occupied_irreps, contracted_irreps, output_irreps):
    own = amplitudes.shape[0]
    block = own * CORES
    slots = block // IRREPS
    sibling = lambda p, m, c: (p, 1 - m, c)

    raw = move(amplitudes, sibling)
    order, key, contracted, outputs, ours, staged = pack(
        occupied_irreps, contracted_irreps, output_irreps, amplitudes, integrals, block
    )
    raw, order, staged = lax.optimization_barrier((raw, order, staged))
    other = move(staged, sibling)
    packed = fold(order, contracted, ours, raw, slots)

    side = move(packed, lambda p, m, c: ((p + 1 + m) % PLACES, 1 - m, c))
    far = move(packed, lambda p, m, c: ((p + 3) % PLACES, 1 - m, c))
    side_too = move(side, sibling)
    masked, other_masked = mask(contracted, staged, other)
    send, send_far, keep = sums(
        (packed, side, side_too, far), masked, other_masked, slots
    )
    got = move(send, lambda p, m, c: (p, m, (c + 2 - m) % COLS))
    got_far = move(send_far, lambda p, m, c: (p, 1 - m, (c + 3) % COLS))
    got_too = move(got[slots:], sibling)
    return expand(keep, got, got_far, got_too, key, outputs)


def solution(mesh):
    small = mesh.shape["row"] == PLACES * CORES and mesh.shape["col"] == COLS
    return jax.shard_map(
        quad if small else general,
        mesh=mesh,
        in_specs=(P("row", "col"), P("col", "row"), P(), P("col"), P("row")),
        out_specs=P("col", "row"),
        check_vma=False,
    )
```

```python
import functools

import jax
import jax.numpy as jnp
from jax import lax
from jax.experimental import pallas as pl
from jax.experimental.pallas import tpu as pltpu
from jax.sharding import PartitionSpec as P

IRREPS = 8
CORES, PLACES, COLS = 2, 4, 4
LABEL_ROWS = 16


def in_hbm(x):
    return pltpu.with_memory_space_constraint(x, pltpu.HBM)


def in_vmem(x):
    return pltpu.with_memory_space_constraint(x, pltpu.VMEM)


def swap(x, axis, mask):
    count = lax.axis_size(axis)
    return lax.ppermute(x, axis, [(i, i ^ mask) for i in range(count)])


def ranks(labels, order):
    same = labels[:, None] == labels[None, :]
    before = order[None, :] < order[:, None]
    return jnp.sum((same & before).astype(jnp.int32), axis=1)


def general(amplitudes, integrals, occupied_irreps, contracted_irreps, output_irreps):
    rows, cols = lax.axis_size("row"), lax.axis_size("col")
    pairs = occupied_irreps.shape[0]
    own = amplitudes.shape[0]
    block = pairs // cols
    slots = block // IRREPS
    share = block // own
    row, col = lax.axis_index("row"), lax.axis_index("col")
    place, member = row // share, row % share

    raw, labels, order = [amplitudes], [], []
    step = 1
    while step < share:
        raw.append(swap(jnp.concatenate(raw, 0), "row", step))
        step *= 2
    raw = jnp.concatenate(raw, 0)
    for j in range(share):
        first = (member ^ j) * own
        labels.append(lax.dynamic_slice_in_dim(occupied_irreps, place * block + first, own, 0))
        order.append(first + jnp.arange(own, dtype=jnp.int32))
    labels, order = jnp.concatenate(labels), jnp.concatenate(order)
    rank = ranks(labels, order)
    pick = (rank[None, :] == jnp.arange(slots, dtype=jnp.int32)[:, None]).astype(jnp.bfloat16)
    kept = jnp.where(labels[:, None] == contracted_irreps[None, :], raw, jnp.zeros_like(raw))
    packed = jnp.dot(pick, kept, preferred_element_type=jnp.float32).astype(jnp.bfloat16)

    step = share
    while step < rows:
        packed = jnp.concatenate([packed, swap(packed, "row", step)], 0)
        step *= 2
    masked = jnp.where(contracted_irreps[:, None] == output_irreps[None, :], integrals, jnp.zeros_like(integrals))
    sums = jnp.dot(packed, masked, preferred_element_type=jnp.float32)
    turn = col ^ place
    parts = [lax.dynamic_slice_in_dim(sums, (turn ^ t) * slots, slots, 0) for t in range(cols)]
    step = 1
    while step < cols:
        got = swap(jnp.concatenate(parts[1::2], 0), "col", step)
        parts = [part + got[t * slots : (t + 1) * slots] for t, part in enumerate(parts[::2])]
        step *= 2
    total = parts[0]

    mine = lax.dynamic_slice_in_dim(occupied_irreps, col * block, block, 0)
    slot = ranks(mine, jnp.arange(block, dtype=jnp.int32))
    out = jnp.zeros((block, total.shape[1]), jnp.float32)
    match = mine[:, None] == output_irreps[None, :]
    for s in range(slots):
        out = jnp.where(match & (slot[:, None] == s), total[s][None, :], out)
    return out


def keys(occupied, place, block):
    slots = block // IRREPS
    labels = jnp.zeros((1, block), jnp.int32)
    for b in range(occupied.shape[1] // block):
        labels = jnp.where(place == b, occupied[:, b * block : (b + 1) * block], labels)
    irrep = lax.broadcasted_iota(jnp.int32, (IRREPS, block), 0)
    same = jnp.where(labels == irrep, 1.0, 0.0)
    lane = lax.broadcasted_iota(jnp.int32, (block, block), 1)
    sublane = lax.broadcasted_iota(jnp.int32, (block, block), 0)
    before = jnp.where(sublane < lane, 1.0, 0.0).astype(jnp.bfloat16)
    counts = jnp.dot(same.astype(jnp.bfloat16), before, preferred_element_type=jnp.float32)
    rank = jnp.sum(same * counts, axis=0, keepdims=True)
    return labels * slots + rank.astype(jnp.int32)


def pack_kernel(block, occupied_ref, contracted_ref, outputs_ref, amplitudes_ref, integrals_ref, order_ref, key_ref, contracted_out, outputs_out, own_out, staged_ref, occupied, sems):
    copies = [
        pltpu.make_async_copy(src, dst, sems.at[n])
        for n, (src, dst) in enumerate(
            (
                (occupied_ref, occupied),
                (contracted_ref, contracted_out),
                (outputs_ref, outputs_out),
                (amplitudes_ref, own_out),
                (integrals_ref, staged_ref.at[pl.ds(0, integrals_ref.shape[0])]),
            )
        )
    ]
    for copy in copies:
        copy.start()
    copies[0].wait()
    key = keys(occupied[...], lax.axis_index("row") // CORES, block)
    sublane = lax.broadcasted_iota(jnp.int32, (block, block), 0)
    order_ref[...] = jnp.where(key == sublane, 1.0, 0.0).astype(jnp.bfloat16)
    key = keys(occupied[...], lax.axis_index("col"), block)
    lane = lax.broadcasted_iota(jnp.int32, (block, block), 1)
    column = jnp.sum(jnp.where(lane == sublane, key, 0), axis=1, keepdims=True)
    key_ref[...] = jnp.broadcast_to(column, key_ref.shape)
    copies[2].wait()
    labels = outputs_out[...].astype(jnp.float32).astype(jnp.bfloat16)
    staged_ref[integrals_ref.shape[0] :] = jnp.broadcast_to(labels, (LABEL_ROWS, labels.shape[1]))
    for copy in (copies[1], *copies[3:]):
        copy.wait()


def pack(occupied_irreps, contracted_irreps, output_irreps, amplitudes, integrals, block):
    rows, depth = amplitudes.shape
    width = output_irreps.shape[0]
    pairs = occupied_irreps.shape[0]
    args = (
        occupied_irreps.reshape(1, pairs),
        contracted_irreps.reshape(1, depth),
        output_irreps.reshape(1, width),
        amplitudes,
        integrals,
    )
    return pl.pallas_call(
        functools.partial(pack_kernel, block),
        out_shape=(
            pltpu.VMEM((block, block), jnp.bfloat16),
            pltpu.VMEM((block, 128), jnp.int32),
            pltpu.VMEM((1, depth), jnp.int32),
            pltpu.VMEM((1, width), jnp.int32),
            pltpu.VMEM((rows, depth), jnp.bfloat16),
            pltpu.VMEM((depth + LABEL_ROWS, width), jnp.bfloat16),
        ),
        in_specs=[pl.BlockSpec(memory_space=pltpu.HBM)] * len(args),
        out_specs=[pl.BlockSpec(memory_space=pltpu.VMEM)] * 6,
        scratch_shapes=[pltpu.VMEM((1, pairs), jnp.int32), pltpu.SemaphoreType.DMA((len(args),))],
        compiler_params=pltpu.CompilerParams(vmem_limit_bytes=8 << 20),
        cost_estimate=pl.CostEstimate(flops=1 << 20, bytes_accessed=1 << 18, transcendentals=0),
        name="pack",
    )(*[in_hbm(x) for x in args])


def fold_kernel(slots, order_ref, contracted_ref, own_ref, raw_ref, packed_ref):
    first = lax.axis_index("row") % CORES == 0
    own, raw = own_ref[...], raw_ref[...]
    rows = jnp.concatenate([jnp.where(first, own, raw), jnp.where(first, raw, own)], axis=0)
    ordered = jnp.dot(order_ref[...], rows, preferred_element_type=jnp.float32)
    contracted = contracted_ref[...]
    packed = jnp.zeros((slots, contracted.shape[1]), jnp.float32)
    for g in range(IRREPS):
        packed = jnp.where(contracted == g, ordered[g * slots : (g + 1) * slots], packed)
    packed_ref[...] = packed.astype(jnp.bfloat16)


def fold(order, contracted, own, raw, slots):
    args = [order, contracted, own, raw]
    return pl.pallas_call(
        functools.partial(fold_kernel, slots),
        out_shape=pltpu.VMEM((slots, own.shape[1]), jnp.bfloat16),
        in_specs=[pl.BlockSpec(memory_space=pltpu.VMEM)] * len(args),
        out_specs=pl.BlockSpec(memory_space=pltpu.VMEM),
        compiler_params=pltpu.CompilerParams(vmem_limit_bytes=8 << 20),
        cost_estimate=pl.CostEstimate(flops=1 << 23, bytes_accessed=1 << 17, transcendentals=0),
        name="fold",
    )(*[in_vmem(x) for x in args])


def mask_kernel(contracted_ref, staged_ref, other_ref, masked_ref, other_masked_ref):
    depth = masked_ref.shape[0]
    size = 128
    lane = lax.broadcasted_iota(jnp.int32, (size, size), 1)
    sublane = lax.broadcasted_iota(jnp.int32, (size, size), 0)
    labels = [ref[depth : depth + 1].astype(jnp.float32) for ref in (staged_ref, other_ref)]
    for n in range(depth // size):
        rows = slice(n * size, (n + 1) * size)
        row = contracted_ref[:, rows].astype(jnp.float32)
        column = jnp.sum(jnp.where(lane == sublane, row, 0.0), axis=1, keepdims=True)
        for label, src, dst in zip(labels, (staged_ref, other_ref), (masked_ref, other_masked_ref)):
            kept = jnp.where(column == label, src[rows].astype(jnp.float32), 0.0)
            dst[rows] = kept.astype(jnp.bfloat16)


def mask(contracted, staged, other):
    depth, width = contracted.shape[1], staged.shape[1]
    return pl.pallas_call(
        mask_kernel,
        out_shape=(pltpu.VMEM((depth, width), jnp.bfloat16),) * 2,
        in_specs=[pl.BlockSpec(memory_space=pltpu.VMEM)] * 3,
        out_specs=[pl.BlockSpec(memory_space=pltpu.VMEM)] * 2,
        compiler_params=pltpu.CompilerParams(vmem_limit_bytes=16 << 20),
        cost_estimate=pl.CostEstimate(flops=1 << 21, bytes_accessed=1 << 22, transcendentals=0),
        name="mask",
    )(*[in_vmem(x) for x in (contracted, staged, other)])


def sums_kernel(slots, blocks_refs, staged_ref, other_ref, send_ref, far_ref, keep_ref):
    row, col = lax.axis_index("row"), lax.axis_index("col")
    place, member = row // CORES, row % CORES
    blocks = [ref[...].astype(jnp.float32) for ref in blocks_refs]

    def block(t):
        back = (place - col - t) % PLACES
        turned = jnp.where((back == 1) | (back == 2), 1 + (back + member) % 2, back)
        chosen = blocks[0]
        for n in range(1, PLACES):
            chosen = jnp.where(turned == n, blocks[n], chosen)
        return chosen

    def product(rows, ref):
        return jnp.dot(rows.astype(jnp.bfloat16), ref[...], preferred_element_type=jnp.float32)

    sent = block(2 - member)
    theirs = product(jnp.concatenate([sent, block(3)], 0), other_ref)
    send_ref[slots:] = theirs[:slots]
    far_ref[...] = theirs[slots:]
    ours = product(jnp.concatenate([sent, block(0)], 0), staged_ref)
    send_ref[:slots] = ours[:slots]
    keep_ref[...] = ours[slots:]


def sums(blocks, staged, other, slots):
    width = staged.shape[1]

    def kernel(b0, b1, b2, b3, *refs):
        sums_kernel(slots, (b0, b1, b2, b3), *refs)

    args = [*blocks, staged, other]
    return pl.pallas_call(
        kernel,
        out_shape=(
            pltpu.VMEM((2 * slots, width), jnp.float32),
            pltpu.VMEM((slots, width), jnp.float32),
            pltpu.VMEM((slots, width), jnp.float32),
        ),
        in_specs=[pl.BlockSpec(memory_space=pltpu.VMEM)] * len(args),
        out_specs=[pl.BlockSpec(memory_space=pltpu.VMEM)] * 3,
        compiler_params=pltpu.CompilerParams(vmem_limit_bytes=16 << 20),
        cost_estimate=pl.CostEstimate(flops=1 << 28, bytes_accessed=1 << 21, transcendentals=0),
        name="sums",
    )(*[in_vmem(x) for x in args])


def expand_kernel(keep_ref, got_ref, far_ref, too_ref, key_ref, outputs_ref, out_ref, staged, sems):
    slots, width = keep_ref.shape
    block = key_ref.shape[0]
    outputs = outputs_ref[...]
    total = (keep_ref[...] + got_ref[:slots]) + (far_ref[...] + too_ref[...])
    pieces = sems.shape[0]
    size = block // pieces
    copies = []
    for n in range(pieces):
        rows = slice(n * size, (n + 1) * size)
        key = key_ref[rows, :1]
        out = jnp.zeros((size, width), jnp.float32)
        for s in range(slots):
            out = jnp.where(key == outputs * slots + s, total[s : s + 1], out)
        staged[rows] = out
        copy = pltpu.make_async_copy(staged.at[rows], out_ref.at[rows], sems.at[n])
        copy.start()
        copies.append(copy)
    for copy in copies:
        copy.wait()


def expand(keep, got, far, too, key, outputs, pieces=2):
    slots, width = keep.shape
    block = key.shape[0]
    args = [keep, got, far, too, key, outputs.reshape(1, width)]
    return pl.pallas_call(
        expand_kernel,
        out_shape=pltpu.HBM((block, width), jnp.float32),
        in_specs=[pl.BlockSpec(memory_space=pltpu.VMEM)] * len(args),
        out_specs=pl.BlockSpec(memory_space=pltpu.HBM),
        scratch_shapes=[pltpu.VMEM((block, width), jnp.float32), pltpu.SemaphoreType.DMA((pieces,))],
        compiler_params=pltpu.CompilerParams(vmem_limit_bytes=8 << 20),
        cost_estimate=pl.CostEstimate(flops=1 << 20, bytes_accessed=1 << 18, transcendentals=0),
        name="expand",
    )(*[in_vmem(x) for x in args])


def move(x, target):
    pairs = []
    for r in range(PLACES * CORES):
        for c in range(COLS):
            place, member, col = target(r // CORES, r % CORES, c)
            pairs.append((r * COLS + c, (place * CORES + member) * COLS + col))
    return lax.ppermute(x, ("row", "col"), pairs)


def quad(amplitudes, integrals, occupied_irreps, contracted_irreps, output_irreps):
    own = amplitudes.shape[0]
    block = own * CORES
    slots = block // IRREPS
    sibling = lambda p, m, c: (p, 1 - m, c)

    raw = move(amplitudes, sibling)
    order, key, contracted, outputs, ours, staged = pack(
        occupied_irreps, contracted_irreps, output_irreps, amplitudes, integrals, block
    )
    raw, order, staged = lax.optimization_barrier((raw, order, staged))
    other = move(staged, sibling)
    packed = fold(order, contracted, ours, raw, slots)

    side = move(packed, lambda p, m, c: ((p + 1 + m) % PLACES, 1 - m, c))
    far = move(packed, lambda p, m, c: ((p + 3) % PLACES, 1 - m, c))
    masked, other_masked = mask(contracted, staged, other)
    side, masked = lax.optimization_barrier((side, masked))
    side_too = move(side, sibling)
    send, send_far, keep = sums(
        (packed, side, side_too, far), masked, other_masked, slots
    )
    got = move(send, lambda p, m, c: (p, m, (c + 2 - m) % COLS))
    got_far = move(send_far, lambda p, m, c: (p, 1 - m, (c + 3) % COLS))
    got_too = move(got[slots:], sibling)
    return expand(keep, got, got_far, got_too, key, outputs)


def solution(mesh):
    small = mesh.shape["row"] == PLACES * CORES and mesh.shape["col"] == COLS
    return jax.shard_map(
        quad if small else general,
        mesh=mesh,
        in_specs=(P("row", "col"), P("col", "row"), P(), P("col"), P("row")),
        out_specs=P("col", "row"),
        check_vma=False,
    )
```
